256 devices in a mesh: tm: 32 (over z, x_hi, core), space: 8 (over x_lo, y).
Axes of the slice: x: 4 (x_hi: 2, x_lo: 2; x = x_hi * 2 + x_lo), y: 4, z: 8, core: 2. Of those that a mesh axis runs over, the one named last changes fastest.
Arguments:
- field: float32 [256, 256, 2048], P('tm', 'space'), may hold values from -3 to 3
- step: float32 [1], replicated, may hold values from 9.9e-05 to 0.001
- mass: float32 [1], replicated, may hold values from 0.02 to 0.05
Outputs:
- field_out: float32 [256, 256, 2048], P('tm', 'space')
The draws below stay inside these ranges and needn't reach their ends.
All inputs are finite; a program needn't handle non-finite values.
Results may differ from the reference program's by a relative error of at most 0.0001.
Values sent between devices are 32-bit elements; how exact they have to be, the bound alone decides.
A program may use at most 64 MiB of HBM per device.

```python
import jax
import jax.numpy as jnp
from jax import lax

NT = 256
NY = 64
NZ = 32
ITERS = 2
NX = 256


def scalar_pair(key):
    mass_key = jax.random.fold_in(key, 7)
    ratio_key = jax.random.fold_in(key, 13)
    mass_value = jax.random.uniform(mass_key, (1,), jnp.float32, 0.02, 0.05)
    step_ratio = jax.random.uniform(ratio_key, (1,), jnp.float32, 0.25, 0.4)
    return (mass_value, step_ratio * mass_value * mass_value)


def draw_step(key, part):
    return scalar_pair(key)[1]


def draw_mass(key, part):
    return scalar_pair(key)[0]


def level_of(stream_key, extent, pieces, smallest, top_value):
    loudness = 1.0
    for dim, shards_of in pieces:
        steps = jax.random.uniform(jax.random.fold_in(jax.random.fold_in(stream_key, 6), dim), (shards_of,), jnp.float32, smallest / len(pieces), top_value / len(pieces))
        loudness = loudness * jnp.repeat(jnp.exp(steps), extent[dim] // shards_of).reshape((-1,) + (1,) * (len(extent) - 1 - dim))
    return loudness


def normal_values(own_key, dims, deviation, limit, pieces=(), kind=jnp.bfloat16):
    array = deviation * jax.random.normal(own_key, dims, jnp.float32)
    if pieces:
        array = array * level_of(own_key, dims, pieces, -0.22, 0.18)
    return jnp.clip(array, -limit, limit).astype(kind)


def setup_inputs(seed: int = 0) -> dict:
    key_of = jax.random.split(jax.random.key(seed), 4)
    field = normal_values(key_of[0], (NT, NX, NY * NZ), 0.7, 3.0, ((0, 32), (1, 8)), jnp.float32)
    step = draw_step(jax.random.fold_in(key_of[3], 71), 0)
    mass = draw_mass(jax.random.fold_in(key_of[3], 71), 0)
    return {"field": field, "step": step, "mass": mass}


def laplacian(field):
    total = jnp.roll(field, 1, axis=0) + jnp.roll(field, -1, axis=0) - 8.0 * field
    padded = jnp.pad(field, ((0, 0), (1, 1), (1, 1), (1, 1)))
    total = total + padded[:, 2:, 1:-1, 1:-1] + padded[:, :-2, 1:-1, 1:-1]
    total = total + padded[:, 1:-1, 2:, 1:-1] + padded[:, 1:-1, :-2, 1:-1]
    total = total + padded[:, 1:-1, 1:-1, 2:] + padded[:, 1:-1, 1:-1, :-2]
    return total


def reference(field, step, mass):
    field = field.reshape(NT, NX, NY, NZ)
    wave = jnp.arange(NT).astype(jnp.float32)
    symbol = mass[0] * mass[0] + 4.0 * jnp.sin(jnp.pi * wave / NT) ** 2
    for turn in range(ITERS):
        force = -laplacian(field) + field - 0.9 * field * field + 0.25 * field * field * field
        planes = jnp.moveaxis(force, 1, 0)

        def solve_plane(plane):
            spectrum = jnp.fft.fft(plane, axis=0) / symbol[:, None, None]
            return jnp.real(jnp.fft.ifft(spectrum, axis=0)).astype(field.dtype)

        update = jnp.moveaxis(lax.map(solve_plane, planes), 0, 1)
        field = field - step[0] * update
    return field.reshape(NT, NX, NY * NZ)
```

```python
import jax
import jax.numpy as jnp
from jax import lax
from jax.sharding import PartitionSpec as P

NZ = 32
ITERS = 2
HIGH = lax.Precision.HIGHEST


def x_neighbours(shard, axis):
    devices = lax.axis_size(axis)
    up = [(i, i + 1) for i in range(devices - 1)]
    down = [(j, i) for i, j in up]
    before = lax.ppermute(shard[:, -1:], axis, up)
    after = lax.ppermute(shard[:, :1], axis, down)
    padded = jnp.concatenate([before, shard, after], axis=1)
    return padded[:, 2:] + padded[:, :-2]


def plane_neighbours(flat, depth):
    width = flat.shape[-1]
    zplace = lax.broadcasted_iota(jnp.int32, (width,), 0) % depth
    padded = jnp.pad(flat, ((0, 0), (0, 0), (depth, depth)))
    total = padded[:, :, 2 * depth :] + padded[:, :, :width]
    upper = padded[:, :, depth + 1 : depth + 1 + width]
    lower = padded[:, :, depth - 1 : depth - 1 + width]
    return total + jnp.where(zplace == depth - 1, 0.0, upper) + jnp.where(zplace == 0, 0.0, lower)


def on_device(field, step, mass):
    slices = field.shape[0]
    blocks = lax.axis_size("tm")
    m = mass[0]
    theta = 2.0 * jnp.arcsinh(0.5 * m)
    kappa = 0.5 / jnp.sinh(theta)
    place = jnp.arange(slices)
    power = lambda k: jnp.exp(-theta * k.astype(jnp.float32))
    moments = jnp.stack([power(slices - 1 - place), power(place)])
    rows = jnp.arange(blocks)
    lag = (rows[:, None] - rows[None, :] - 1) % blocks
    whole = -jnp.expm1(-theta * (slices * blocks))
    left = power(slices * lag) / whole
    mix = jnp.zeros((blocks, 2, blocks, 2), jnp.float32)
    mix = mix.at[:, 0, :, 0].set(left).at[:, 1, :, 1].set(left.T).reshape(2 * blocks, 2 * blocks)
    inner = kappa * power(jnp.abs(place[:, None] - place[None, :]))
    edges = kappa * jnp.stack([power(place + 1), power(slices - place)], axis=1)
    flat = field
    for turn in range(ITERS):
        near = x_neighbours(flat, "space") + plane_neighbours(flat, NZ)
        g = flat * ((7.0 - m * m) + flat * (0.25 * flat - 0.9)) - near
        own = jnp.einsum("ms,sab->mab", moments, g, precision=HIGH)
        every = lax.all_to_all(own, "tm", split_axis=1, concat_axis=0, tiled=True)
        mixed = jnp.einsum("pq,qab->pab", mix, every, precision=HIGH)
        ends = lax.all_to_all(mixed, "tm", split_axis=0, concat_axis=1, tiled=True)
        solved = jnp.einsum("ts,sab->tab", inner, g, precision=HIGH)
        solved = solved + jnp.einsum("tm,mab->tab", edges, ends, precision=HIGH)
        flat = flat - step[0] * (flat + solved)
    return flat


def solution(mesh):
    return jax.shard_map(
        on_device,
        mesh=mesh,
        in_specs=(P("tm", "space", None), P(), P()),
        out_specs=P("tm", "space", None),
        check_vma=False,
    )
```

```python
import functools

import jax
import jax.numpy as jnp
from jax import lax
from jax.experimental import pallas as pl
from jax.experimental.pallas import tpu as pltpu
from jax.sharding import PartitionSpec as P

NZ = 32
ITERS = 2
LANES = 128
ROWS = 8
MESH = pl.DeviceIdType.MESH


def kernel(nz, ny, nc, slices, step_ref, mass_ref, field, out, fb, gb, hb, mom, u1, xs, xr, zs, zr, ws, wr, vs, vr, cs, yv,
           load_sem, store_sem, send, recv, hsend, hrecv):
    tiles = fb.shape[1] - 2
    groups = fb.shape[2] // ROWS
    kt = tiles // nc
    tm, sp = lax.axis_index("tm"), lax.axis_index("space")
    z, h, c = tm // 4, (tm // 2) % 2, tm % 2
    lo, y = sp // ny, sp % ny
    last = 2 * ny - 1
    other = (tm + 1 - 2 * c, sp)
    side = lambda hd: (z * 4 + hd * 2 + c, (1 - lo) * ny + y)
    along = lambda d: ((tm + 4 * d) % (4 * nz), sp)
    has_left, has_right = sp > 0, sp < last

    barrier = pltpu.get_barrier_semaphore()

    def greet(device):
        pl.semaphore_signal(barrier, inc=1, device_id=device, device_id_type=MESH)

    greet(other)
    greet(side(0))
    greet(side(1))
    for d in range(1, nz):
        greet(along(d))

    @pl.when(has_left)
    def _():
        greet((tm, sp - 1))

    @pl.when(has_right)
    def _():
        greet((tm, sp + 1))

    loads = [
        pltpu.make_async_copy(
            field.at[:, :, pl.ds(k * LANES, LANES)], fb.at[:, k + 1], load_sem.at[k]
        )
        for k in range(tiles)
    ]
    for load in loads:
        load.start()

    full = lambda value: jnp.full((ROWS, LANES), value, jnp.float32)
    blank = full(0.0)

    @pl.loop(0, slices)
    def _(t):
        for i in range(groups):
            fb[t, 0, pl.ds(i * ROWS, ROWS), :] = blank
            fb[t, tiles + 1, pl.ds(i * ROWS, ROWS), :] = blank

    def clear(which):
        @pl.loop(0, slices)
        def _(t):
            for it in range(ITERS):
                for ch in range(nc):
                    for k in range(kt):
                        hb[it, which, ch, t, k] = blank

    pl.when(jnp.logical_not(has_left))(lambda: clear(0))
    pl.when(jnp.logical_not(has_right))(lambda: clear(1))

    m = full(mass_ref[0])
    s = full(step_ref[0])
    m2 = m * m
    q = m * jnp.sqrt(1.0 + 0.25 * m2) - 0.5 * m2
    double = lambda p: p * (2.0 - p)
    r = 1.0 - q
    q8 = double(double(double(q)))
    q16 = double(q8)
    q32 = double(q16)
    r8, r16, r32 = 1.0 - q8, 1.0 - q16, 1.0 - q32
    whole = q32
    for _ in range((nz - 1).bit_length()):
        whole = double(whole)
    inv = 1.0 / whole
    linear = 7.0 - m2
    keep = 1.0 - s
    gain = s * r / (q * (1.0 + r))
    first = c == 0
    one = full(1.0)
    wa, wb = jnp.where(first, r8, one), jnp.where(first, one, r8)
    za, zb = jnp.where(first, one, blank), jnp.where(first, blank, one)

    lane = lax.broadcasted_iota(jnp.int32, (ROWS, LANES), 1)
    row = lax.broadcasted_iota(jnp.int32, (ROWS, LANES), 0)
    zplace = lane % NZ
    at_first, at_last = zplace == 0, zplace == NZ - 1
    low, high = lane < NZ, lane >= LANES - NZ
    top, bottom = row == 0, row == ROWS - 1

    def stencil(it, ch, which):
        @pl.loop(0, kt)
        def _(k):
            kk = ch * kt + k
            for i in which:
                rows = pl.ds(i * ROWS, ROWS)
                gs = []
                for t in range(slices):
                    f = fb[t, kk + 1, rows, :]
                    if i == 0:
                        xm = jnp.where(top, hb[it, 0, ch, t, k], pltpu.roll(f, 1, 0))
                    else:
                        xm = fb[t, kk + 1, pl.ds(i * ROWS - 1, ROWS), :]
                    if i == groups - 1:
                        xp = jnp.where(bottom, hb[it, 1, ch, t, k], pltpu.roll(f, ROWS - 1, 0))
                    else:
                        xp = fb[t, kk + 1, pl.ds(i * ROWS + 1, ROWS), :]
                    yp = pltpu.roll(jnp.where(low, fb[t, kk + 2, rows, :], f), LANES - NZ, 1)
                    ym = pltpu.roll(jnp.where(high, fb[t, kk, rows, :], f), NZ, 1)
                    zp = pltpu.roll(jnp.where(at_first, 0.0, f), LANES - 1, 1)
                    zm = pltpu.roll(jnp.where(at_last, 0.0, f), 1, 1)
                    near = (xm + xp) + (yp + ym) + (zp + zm)
                    g = f * (linear + f * (0.25 * f - 0.9)) - near
                    gb[t, kk, rows, :] = g
                    gs.append(g)
                before, after = gs[0], gs[-1]
                for t in range(1, slices):
                    before = r * before + gs[t]
                    after = r * after + gs[slices - 1 - t]
                mom[it, ch, i // 2, i % 2, 0, k] = before
                mom[it, ch, i // 2, i % 2, 1, k] = after

    def solve(it, ch):
        @pl.loop(0, kt)
        def _(k):
            kk = ch * kt + k
            for i in range(groups):
                rows = pl.ds(i * ROWS, ROWS)
                gs = [gb[t, kk, rows, :] for t in range(slices)]
                state = yv[it, ch, i // 2, i % 2, 0, k]
                states = []
                for t in range(slices):
                    state = r * state + gs[t]
                    states.append(state)
                ahead = r * yv[it, ch, i // 2, i % 2, 1, k]
                for t in reversed(range(slices)):
                    f = fb[t, kk + 1, rows, :]
                    fb[t, kk + 1, rows, :] = keep * f - gain * (states[t] + ahead)
                    ahead = r * (gs[t] + ahead)

    pending = []

    def copy(src, dst, send_sem, recv_sem, device):
        return pltpu.make_async_remote_copy(
            src_ref=src, dst_ref=dst, send_sem=send_sem, recv_sem=recv_sem, device_id=device, device_id_type=MESH
        )

    def start(src, dst, it, ch, a, b, device):
        one_copy = copy(src, dst, send.at[it, ch, a], recv.at[it, ch, b], device)
        one_copy.start()
        pending.append(one_copy)

    def arrive(dst, it, ch, b):
        copy(dst, dst, send.at[it, ch, b], recv.at[it, ch, b], other).wait_recv()

    def halo(it, ch, which):
        row_from, row_to = (groups * ROWS - 1, 0) if which == 0 else (0, ROWS - 1)
        return copy(
            fb.at[:, pl.ds(1 + ch * kt, kt), pl.ds(row_from, 1), :],
            hb.at[it, which, ch, :, :, pl.ds(row_to, 1), :],
            hsend.at[it, which, ch],
            hrecv.at[it, which, ch],
            (tm, sp + 1) if which == 0 else (tm, sp - 1),
        )

    def send_halo(it, ch):
        pl.when(has_right)(lambda: halo(it, ch, 0).start())
        pl.when(has_left)(lambda: halo(it, ch, 1).start())

    def sent_halo(it, ch):
        pl.when(has_right)(lambda: halo(it, ch, 0).wait_send())
        pl.when(has_left)(lambda: halo(it, ch, 1).wait_send())

    def wait_halo(it, ch):
        pl.when(has_left)(lambda: halo(it, ch, 0).wait_recv())
        pl.when(has_right)(lambda: halo(it, ch, 1).wait_recv())

    def up_core(it, ch):
        start(mom.at[it, ch, 1 - c], u1.at[it, ch], it, ch, 0, 0, other)

    def up_side(it, ch):
        arrive(u1.at[it, ch], it, ch, 0)

        @pl.loop(0, kt)
        def _(k):
            for hd in range(2):
                xs[it, ch, hd, 0, k] = wa * mom[it, ch, c, hd, 0, k] + wb * u1[it, ch, hd, 0, k]
                xs[it, ch, hd, 1, k] = wb * mom[it, ch, c, hd, 1, k] + wa * u1[it, ch, hd, 1, k]

        for hd in range(2):
            start(xs.at[it, ch, hd], xr.at[it, ch, h], it, ch, 1 + hd, 1 + h, side(hd))

    far_first = sorted(range(1, nz), key=lambda d: (-min(d, nz - d), d))

    def up_along(it, ch):
        for hs in range(2):
            arrive(xr.at[it, ch, hs], it, ch, 1 + hs)

        @pl.loop(0, kt)
        def _(k):
            zs[it, ch, k, 0] = r16 * xr[it, ch, 0, 0, k] + xr[it, ch, 1, 0, k]
            zs[it, ch, k, 1] = xr[it, ch, 0, 1, k] + r16 * xr[it, ch, 1, 1, k]

        for d in far_first:
            start(zs.at[it, ch, (z + d) % nz], zr.at[it, ch, z], it, ch, 2 + d, 2 + d, along(d))
        zr[it, ch, z] = zs[it, ch, z]

    def down_along(it, ch):
        for d in far_first:
            arrive(zr.at[it, ch, (z + nz - d) % nz], it, ch, 2 + d)
        ms = [zr[it, ch, j, 0] for j in range(nz)]
        ns = [zr[it, ch, j, 1] for j in range(nz)]
        before, after = ms[0], ns[-1]
        for j in range(1, nz):
            before = r32 * before + ms[j]
            after = r32 * after + ns[nz - 1 - j]
        before, after = inv * before, inv * after
        for j in range(nz):
            ws[it, ch, j, 0] = before
            ws[it, ch, nz - 1 - j, 1] = after
            before = r32 * before + ms[j]
            after = r32 * after + ns[nz - 1 - j]
        for d in far_first:
            start(ws.at[it, ch, (z + d) % nz], wr.at[it, ch, z], it, ch, 1 + nz + d, 1 + nz + d, along(d))
        wr[it, ch, z] = ws[it, ch, z]

    def down_side(it, ch):
        for d in far_first:
            arrive(wr.at[it, ch, (z + nz - d) % nz], it, ch, 1 + nz + d)

        @pl.loop(0, kt)
        def _(k):
            before, after = wr[it, ch, k, 0], wr[it, ch, k, 1]
            vs[it, ch, 0, 0, k] = before
            vs[it, ch, 0, 1, k] = xr[it, ch, 1, 1, k] + r16 * after
            vs[it, ch, 1, 0, k] = xr[it, ch, 0, 0, k] + r16 * before
            vs[it, ch, 1, 1, k] = after

        for hd in range(2):
            start(vs.at[it, ch, hd], vr.at[it, ch, h], it, ch, 1 + 2 * nz + hd, 1 + 2 * nz + h, side(hd))

    def down_core(it, ch):
        for hs in range(2):
            arrive(vr.at[it, ch, hs], it, ch, 1 + 2 * nz + hs)

        @pl.loop(0, kt)
        def _(k):
            for hd in range(2):
                before, after = vr[it, ch, hd, 0, k], vr[it, ch, hd, 1, k]
                cs[it, ch, hd, 0, k] = wa * before + za * mom[it, ch, c, hd, 0, k]
                cs[it, ch, hd, 1, k] = wb * after + zb * mom[it, ch, c, hd, 1, k]
                yv[it, ch, c, hd, 0, k] = wb * before + zb * u1[it, ch, hd, 0, k]
                yv[it, ch, c, hd, 1, k] = wa * after + za * u1[it, ch, hd, 1, k]

        start(cs.at[it, ch], yv.at[it, ch, c], it, ch, 3 + 2 * nz, 3 + 2 * nz, other)

    inner, outer = tuple(range(1, groups - 1)), (0, groups - 1)
    for load in loads:
        load.wait()
    stores = []
    for it in range(ITERS):
        if it == 0:
            stencil(it, 0, inner)
            pl.semaphore_wait(barrier, nz + 2 + has_left.astype(jnp.int32) + has_right.astype(jnp.int32))
            for ch in range(nc):
                send_halo(it, ch)
        else:
            stencil(it, 0, inner)
        for ch in range(1, nc):
            stencil(it, ch, inner)
        for ch in range(nc):
            wait_halo(it, ch)
            stencil(it, ch, outer)
            up_core(it, ch)
        for phase in (up_side, up_along, down_along, down_side, down_core):
            for ch in range(nc):
                phase(it, ch)
        for ch in range(nc):
            arrive(yv.at[it, ch, 1 - c], it, ch, 3 + 2 * nz)
            sent_halo(it, ch)
            solve(it, ch)
            if it + 1 < ITERS:
                send_halo(it + 1, ch)
            else:
                for k in range(ch * kt, (ch + 1) * kt):
                    store = pltpu.make_async_copy(
                        fb.at[:, k + 1], out.at[:, :, pl.ds(k * LANES, LANES)], store_sem.at[k]
                    )
                    store.start()
                    stores.append(store)
    for one_copy in pending:
        one_copy.wait_send()
    for store in stores:
        store.wait()


def solution(mesh):
    nz = mesh.shape["tm"] // 4
    ny = mesh.shape["space"] // 2

    def on_device(field, step, mass):
        slices, planes, width = field.shape
        tiles = width // LANES
        nc = tiles // nz
        groups = planes // ROWS
        tile = (ROWS, LANES)
        vmem = lambda *shape: pltpu.VMEM(shape, jnp.float32)
        level = (ITERS, nc)
        sems = 4 + 2 * nz
        return pl.pallas_call(
            functools.partial(kernel, nz, ny, nc, slices),
            out_shape=jax.ShapeDtypeStruct(field.shape, field.dtype),
            in_specs=[
                pl.BlockSpec(memory_space=pltpu.SMEM),
                pl.BlockSpec(memory_space=pltpu.SMEM),
                pl.BlockSpec(memory_space=pl.ANY),
            ],
            out_specs=pl.BlockSpec(memory_space=pl.ANY),
            scratch_shapes=[
                vmem(slices, tiles + 2, planes, LANES),
                vmem(slices, tiles, planes, LANES),
                vmem(ITERS, 2, nc, slices, nz, *tile),
                vmem(*level, 2, 2, 2, nz, *tile),
                vmem(*level, 2, 2, nz, *tile),
                vmem(*level, 2, 2, nz, *tile),
                vmem(*level, 2, 2, nz, *tile),
                vmem(*level, nz, 2, *tile),
                vmem(*level, nz, 2, *tile),
                vmem(*level, nz, 2, *tile),
                vmem(*level, nz, 2, *tile),
                vmem(*level, 2, 2, nz, *tile),
                vmem(*level, 2, 2, nz, *tile),
                vmem(*level, 2, 2, nz, *tile),
                vmem(*level, 2, 2, 2, nz, *tile),
                pltpu.SemaphoreType.DMA((tiles,)),
                pltpu.SemaphoreType.DMA((tiles,)),
                pltpu.SemaphoreType.DMA((*level, sems)),
                pltpu.SemaphoreType.DMA((*level, sems)),
                pltpu.SemaphoreType.DMA((ITERS, 2, nc)),
                pltpu.SemaphoreType.DMA((ITERS, 2, nc)),
            ],
            compiler_params=pltpu.CompilerParams(
                collective_id=0, has_side_effects=True, vmem_limit_bytes=48 * 1024 * 1024
            ),
        )(step, mass, field)

    return jax.shard_map(
        on_device,
        mesh=mesh,
        in_specs=(P("tm", "space", None), P(), P()),
        out_specs=P("tm", "space", None),
        check_vma=False,
    )
```

```python
import functools

import jax
import jax.numpy as jnp
from jax import lax
from jax.experimental import pallas as pl
from jax.experimental.pallas import tpu as pltpu
from jax.sharding import PartitionSpec as P

NZ = 32
ITERS = 2
VMEM_MIB = 40
LANES = 128
ROWS = 8
MESH = pl.DeviceIdType.MESH


def kernel(nz, ny, slices, step_ref, mass_ref, field, out, fb, gb, hs, hb, mom, u1, xs, zr, ws, wr, cs, yv,
           load_sem, send, recv, hsend, hrecv):
    tiles = fb.shape[1] - 2
    groups = fb.shape[2] // ROWS
    tm, sp = lax.axis_index("tm"), lax.axis_index("space")
    z, h, c = tm // 4, (tm // 2) % 2, tm % 2
    lo, y = sp // ny, sp % ny
    last = 2 * ny - 1
    other = (tm + 1 - 2 * c, sp)
    owner = lambda d, hd: (((z + d) % nz) * 4 + hd * 2 + c, (1 - lo) * ny + y)
    has_left, has_right = sp > 0, sp < last

    barrier = pltpu.get_barrier_semaphore()

    def greet(device):
        pl.semaphore_signal(barrier, inc=1, device_id=device, device_id_type=MESH)

    far_first = sorted(range(nz), key=lambda d: (-min(d, nz - d), d))
    for d in far_first:
        for hd in range(2):
            greet(owner(d, hd))
    greet(other)

    @pl.when(has_left)
    def _():
        greet((tm, sp - 1))

    @pl.when(has_right)
    def _():
        greet((tm, sp + 1))

    loads = [
        pltpu.make_async_copy(
            field.at[:, :, pl.ds(k * LANES, LANES)], fb.at[:, k + 1], load_sem.at[k]
        )
        for k in range(tiles)
    ]
    for load in loads:
        load.start()

    full = lambda value: jnp.full((ROWS, LANES), value, jnp.float32)
    blank = full(0.0)

    for t in range(slices):
        for i in range(groups):
            fb[t, 0, pl.ds(i * ROWS, ROWS), :] = blank
            fb[t, tiles + 1, pl.ds(i * ROWS, ROWS), :] = blank

    def clear(which):
        for it in range(ITERS):
            hb[it, which] = jnp.zeros(hb.shape[2:], jnp.float32)

    pl.when(jnp.logical_not(has_left))(lambda: clear(0))
    pl.when(jnp.logical_not(has_right))(lambda: clear(1))

    m = full(mass_ref[0])
    s = full(step_ref[0])
    m2 = m * m
    q = m * jnp.sqrt(1.0 + 0.25 * m2) - 0.5 * m2
    double = lambda p: p * (2.0 - p)
    r = 1.0 - q
    q8 = double(double(double(q)))
    q16 = double(q8)
    r8, r16 = 1.0 - q8, 1.0 - q16
    whole = q16
    for _ in range((2 * nz - 1).bit_length()):
        whole = double(whole)
    inv = 1.0 / whole
    linear = 7.0 - m2
    keep = 1.0 - s
    gain = s * r / (q * (1.0 + r))
    first = c == 0
    one = full(1.0)
    wa, wb = jnp.where(first, r8, one), jnp.where(first, one, r8)
    za, zb = jnp.where(first, one, blank), jnp.where(first, blank, one)

    lane = lax.broadcasted_iota(jnp.int32, (ROWS, LANES), 1)
    row = lax.broadcasted_iota(jnp.int32, (ROWS, LANES), 0)
    zplace = lane % NZ
    at_first, at_last = zplace == 0, zplace == NZ - 1
    low, high = lane < NZ, lane >= LANES - NZ
    top, bottom = row == 0, row == ROWS - 1

    parts = (tuple(range(1, groups - 1)), (0, groups - 1))

    def stencil(it, part):
        @pl.loop(0, tiles // 4)
        def _(quad):
            for k in (quad * 4 + j for j in range(4)):
                for half, i in enumerate(parts[part]):
                    rows = pl.ds(i * ROWS, ROWS)
                    gs = []
                    for t in range(slices):
                        f = fb[t, k + 1, rows, :]
                        if i == 0:
                            xm = jnp.where(top, hb[it, 0, t, pl.ds(k, 1), :], pltpu.roll(f, 1, 0))
                        else:
                            xm = fb[t, k + 1, pl.ds(i * ROWS - 1, ROWS), :]
                        if i == groups - 1:
                            xp = jnp.where(bottom, hb[it, 1, t, pl.ds(k, 1), :], pltpu.roll(f, ROWS - 1, 0))
                        else:
                            xp = fb[t, k + 1, pl.ds(i * ROWS + 1, ROWS), :]
                        yp = pltpu.roll(jnp.where(low, fb[t, k + 2, rows, :], f), LANES - NZ, 1)
                        ym = pltpu.roll(jnp.where(high, fb[t, k, rows, :], f), NZ, 1)
                        zp = pltpu.roll(jnp.where(at_first, 0.0, f), LANES - 1, 1)
                        zm = pltpu.roll(jnp.where(at_last, 0.0, f), 1, 1)
                        near = (xm + xp) + (yp + ym) + (zp + zm)
                        g = f * (linear + f * (0.25 * f - 0.9)) - near
                        gb[t, k, rows, :] = g
                        gs.append(g)
                    before, after = gs[0], gs[-1]
                    for t in range(1, slices):
                        before = r * before + gs[t]
                        after = r * after + gs[slices - 1 - t]
                    mom[it, part, half, k, 0] = before
                    mom[it, part, half, k, 1] = after

    def solve(it, part):
        @pl.loop(0, tiles // 4)
        def _(quad):
            for j in range(4):
                k = quad * 4 + j
                for half, i in enumerate(parts[part]):
                    rows = pl.ds(i * ROWS, ROWS)
                    gs = [gb[t, k, rows, :] for t in range(slices)]
                    state = yv[it, part, half, k, 0]
                    states = []
                    for t in range(slices):
                        state = r * state + gs[t]
                        states.append(state)
                    ahead = r * yv[it, part, half, k, 1]
                    for t in reversed(range(slices)):
                        new = keep * fb[t, k + 1, rows, :] - gain * (states[t] + ahead)
                        if it + 1 < ITERS:
                            fb[t, k + 1, rows, :] = new
                        else:
                            out[t, rows, pl.ds(pl.multiple_of(k * LANES, LANES), LANES)] = new
                        if it + 1 < ITERS and i == 0:
                            hs[it + 1, 1, t, pl.ds(k, 1), :] = new[:1]
                        if it + 1 < ITERS and i == groups - 1:
                            hs[it + 1, 0, t, pl.ds(k, 1), :] = new[ROWS - 1 :]
                        ahead = r * (gs[t] + ahead)

    pending = []

    def copy(src, dst, send_sem, recv_sem, device):
        return pltpu.make_async_remote_copy(
            src_ref=src, dst_ref=dst, send_sem=send_sem, recv_sem=recv_sem, device_id=device, device_id_type=MESH
        )

    def start(src, dst, it, part, a, b, device):
        one_copy = copy(src, dst, send.at[it, part, a], recv.at[it, part, b], device)
        one_copy.start()
        pending.append(one_copy)

    def arrive(dst, it, part, b):
        copy(dst, dst, send.at[it, part, b], recv.at[it, part, b], other).wait_recv()

    def pack(it):
        @pl.loop(0, slices)
        def _(t):
            for which, edge in enumerate((groups * ROWS - 1, 0)):
                for k in range(tiles):
                    hs[it, which, t, pl.ds(k, 1), :] = fb[t, k + 1, pl.ds(edge, 1), :]

    def halo(it, which):
        return copy(
            hs.at[it, which],
            hb.at[it, which],
            hsend.at[it, which],
            hrecv.at[it, which],
            (tm, sp + 1) if which == 0 else (tm, sp - 1),
        )

    def send_halo(it):
        pl.when(has_right)(lambda: halo(it, 0).start())
        pl.when(has_left)(lambda: halo(it, 1).start())

    def wait_halo(it):
        pl.when(has_left)(lambda: halo(it, 0).wait_recv())
        pl.when(has_right)(lambda: halo(it, 1).wait_recv())

    up = lambda d, hd: 1 + 2 * d + hd
    down = lambda d, hd: 1 + 2 * nz + 2 * d + hd
    back = 1 + 4 * nz

    def up_core(it, part):
        start(mom.at[it, part, 1 - c], u1.at[it, part], it, part, 0, 0, other)

    def up_owner(it, part):
        arrive(u1.at[it, part], it, part, 0)
        for k in range(tiles):
            xs[it, part, k, 0] = wa * mom[it, part, c, k, 0] + wb * u1[it, part, k, 0]
            xs[it, part, k, 1] = wb * mom[it, part, c, k, 1] + wa * u1[it, part, k, 1]
        for d in far_first:
            for hd in range(2):
                src = xs.at[it, part, hd * nz + (z + d) % nz]
                start(src, zr.at[it, part, z * 2 + h], it, part, up(d, hd), up(d, h), owner(d, hd))

    def down_owner(it, part):
        for d in reversed(far_first):
            for hd in range(2):
                arrive(zr.at[it, part, ((z + nz - d) % nz) * 2 + hd], it, part, up(d, hd))
        ms = [zr[it, part, j, 0] for j in range(2 * nz)]
        ns = [zr[it, part, j, 1] for j in range(2 * nz)]
        left, right, ratio = ms, ns, r16
        while len(left) > 1:
            pairs = range(0, len(left), 2)
            left = [ratio * left[j] + left[j + 1] for j in pairs]
            right = [right[j] + ratio * right[j + 1] for j in pairs]
            ratio = ratio * ratio
        before, after = inv * left[0], inv * right[0]
        for j in range(2 * nz):
            ws[it, part, j, 0] = before
            ws[it, part, 2 * nz - 1 - j, 1] = after
            before = r16 * before + ms[j]
            after = r16 * after + ns[2 * nz - 1 - j]
        for d in far_first:
            for hd in range(2):
                src = ws.at[it, part, ((z + d) % nz) * 2 + hd]
                start(src, wr.at[it, part, h * nz + z], it, part, down(d, hd), down(d, h), owner(d, hd))

    def down_core(it, part):
        for d in reversed(far_first):
            for hd in range(2):
                arrive(wr.at[it, part, hd * nz + (z + nz - d) % nz], it, part, down(d, hd))
        for k in range(tiles):
            before, after = wr[it, part, k, 0], wr[it, part, k, 1]
            cs[it, part, k, 0] = wa * before + za * mom[it, part, c, k, 0]
            cs[it, part, k, 1] = wb * after + zb * mom[it, part, c, k, 1]
        start(cs.at[it, part], yv.at[it, part, c], it, part, back, back, other)
        for k in range(tiles):
            before, after = wr[it, part, k, 0], wr[it, part, k, 1]
            yv[it, part, c, k, 0] = wb * before + zb * u1[it, part, k, 0]
            yv[it, part, c, k, 1] = wa * after + za * u1[it, part, k, 1]

    for load in loads:
        load.wait()
    pack(0)
    stencil(0, 0)
    pl.semaphore_wait(barrier, 2 * nz + 1 + has_left.astype(jnp.int32) + has_right.astype(jnp.int32))
    send_halo(0)
    for it in range(ITERS):
        up_core(it, 0)
        wait_halo(it)
        stencil(it, 1)
        up_core(it, 1)
        for phase in (up_owner, down_owner, down_core):
            for part in range(2):
                phase(it, part)
        for part in range(2):
            arrive(yv.at[it, part, 1 - c], it, part, back)
            solve(it, part)
        if it + 1 < ITERS:
            send_halo(it + 1)
            stencil(it + 1, 0)
    for one_copy in pending:
        one_copy.wait_send()
    for it in range(ITERS):
        pl.when(has_right)(lambda: halo(it, 0).wait_send())
        pl.when(has_left)(lambda: halo(it, 1).wait_send())


def solution(mesh):
    nz = mesh.shape["tm"] // 4
    ny = mesh.shape["space"] // 2

    def on_device(field, step, mass):
        slices, planes, width = field.shape
        tiles = width // LANES
        tile = (ROWS, LANES)
        vmem = lambda *shape: pltpu.VMEM(shape, jnp.float32)
        level = (ITERS, 2)
        sems = 2 + 4 * nz
        return pl.pallas_call(
            functools.partial(kernel, nz, ny, slices),
            out_shape=jax.ShapeDtypeStruct(field.shape, field.dtype),
            in_specs=[
                pl.BlockSpec(memory_space=pltpu.SMEM),
                pl.BlockSpec(memory_space=pltpu.SMEM),
                pl.BlockSpec(memory_space=pltpu.HBM),
            ],
            out_specs=pl.BlockSpec(memory_space=pltpu.VMEM),
            scratch_shapes=[
                vmem(slices, tiles + 2, planes, LANES),
                vmem(slices, tiles, planes, LANES),
                vmem(ITERS, 2, slices, tiles, LANES),
                vmem(ITERS, 2, slices, tiles, LANES),
                vmem(*level, 2, tiles, 2, *tile),
                vmem(*level, tiles, 2, *tile),
                vmem(*level, tiles, 2, *tile),
                vmem(*level, tiles, 2, *tile),
                vmem(*level, tiles, 2, *tile),
                vmem(*level, tiles, 2, *tile),
                vmem(*level, tiles, 2, *tile),
                vmem(*level, 2, tiles, 2, *tile),
                pltpu.SemaphoreType.DMA((tiles,)),
                pltpu.SemaphoreType.DMA((*level, sems)),
                pltpu.SemaphoreType.DMA((*level, sems)),
                pltpu.SemaphoreType.DMA((ITERS, 2)),
                pltpu.SemaphoreType.DMA((ITERS, 2)),
            ],
            compiler_params=pltpu.CompilerParams(
                collective_id=0, has_side_effects=True, vmem_limit_bytes=VMEM_MIB * 1024 * 1024
            ),
        )(step, mass, field)

    return jax.shard_map(
        on_device,
        mesh=mesh,
        in_specs=(P("tm", "space", None), P(), P()),
        out_specs=P("tm", "space", None),
        check_vma=False,
    )
```

```python
import functools

import jax
import jax.numpy as jnp
from jax import lax
from jax.experimental import pallas as pl
from jax.experimental.pallas import tpu as pltpu
from jax.sharding import PartitionSpec as P

NZ = 32
ITERS = 2
VMEM_MIB = 40
LANES = 128
ROWS = 8
MESH = pl.DeviceIdType.MESH


def kernel(nz, ny, slices, step_ref, mass_ref, field, out, fb, gb, hs, hb, mom, u1, xs, zr, ws, wr, cs, yv,
           load_sem, send, recv, hsend, hrecv):
    tiles = fb.shape[1] - 2
    groups = fb.shape[2] // ROWS
    tm, sp = lax.axis_index("tm"), lax.axis_index("space")
    z, h, c = tm // 4, (tm // 2) % 2, tm % 2
    lo, y = sp // ny, sp % ny
    last = 2 * ny - 1
    other = (tm + 1 - 2 * c, sp)
    owner = lambda d, hd: (((z + d) % nz) * 4 + hd * 2 + c, (1 - lo) * ny + y)
    has_left, has_right = sp > 0, sp < last

    barrier = pltpu.get_barrier_semaphore()

    def greet(device):
        pl.semaphore_signal(barrier, inc=1, device_id=device, device_id_type=MESH)

    far_first = sorted(range(nz), key=lambda d: (-min(d, nz - d), d))
    for d in far_first:
        for hd in range(2):
            greet(owner(d, hd))
    greet(other)

    @pl.when(has_left)
    def _():
        greet((tm, sp - 1))

    @pl.when(has_right)
    def _():
        greet((tm, sp + 1))

    loads = [
        pltpu.make_async_copy(
            field.at[:, :, pl.ds(k * LANES, LANES)], fb.at[:, k + 1], load_sem.at[k]
        )
        for k in range(tiles)
    ]
    for load in loads:
        load.start()

    full = lambda value: jnp.full((ROWS, LANES), value, jnp.float32)
    blank = full(0.0)

    for t in range(slices):
        for i in range(groups):
            fb[t, 0, pl.ds(i * ROWS, ROWS), :] = blank
            fb[t, tiles + 1, pl.ds(i * ROWS, ROWS), :] = blank

    def clear(which):
        for it in range(ITERS):
            hb[it, which] = jnp.zeros(hb.shape[2:], jnp.float32)

    pl.when(jnp.logical_not(has_left))(lambda: clear(0))
    pl.when(jnp.logical_not(has_right))(lambda: clear(1))

    m = full(mass_ref[0])
    s = full(step_ref[0])
    m2 = m * m
    q = m * jnp.sqrt(1.0 + 0.25 * m2) - 0.5 * m2
    double = lambda p: p * (2.0 - p)
    r = 1.0 - q
    q8 = double(double(double(q)))
    q16 = double(q8)
    r8, r16 = 1.0 - q8, 1.0 - q16
    whole = q16
    for _ in range((2 * nz - 1).bit_length()):
        whole = double(whole)
    inv = 1.0 / whole
    linear = 7.0 - m2
    keep = 1.0 - s
    gain = s * r / (q * (1.0 + r))
    first = c == 0
    one = full(1.0)
    wa, wb = jnp.where(first, r8, one), jnp.where(first, one, r8)
    za, zb = jnp.where(first, one, blank), jnp.where(first, blank, one)

    lane = lax.broadcasted_iota(jnp.int32, (ROWS, LANES), 1)
    row = lax.broadcasted_iota(jnp.int32, (ROWS, LANES), 0)
    zplace = lane % NZ
    at_first, at_last = zplace == 0, zplace == NZ - 1
    low, high = lane < NZ, lane >= LANES - NZ
    top, bottom = row == 0, row == ROWS - 1

    parts = (tuple(range(1, groups - 1)), (0, groups - 1))

    def stencil(it, part):
        @pl.loop(0, tiles // 4)
        def _(quad):
            for k in (quad * 4 + j for j in range(4)):
                for half, i in enumerate(parts[part]):
                    rows = pl.ds(i * ROWS, ROWS)
                    gs = []
                    for t in range(slices):
                        f = fb[t, k + 1, rows, :]
                        if i == 0:
                            xm = jnp.where(top, hb[it, 0, t, pl.ds(k, 1), :], pltpu.roll(f, 1, 0))
                        else:
                            xm = fb[t, k + 1, pl.ds(i * ROWS - 1, ROWS), :]
                        if i == groups - 1:
                            xp = jnp.where(bottom, hb[it, 1, t, pl.ds(k, 1), :], pltpu.roll(f, ROWS - 1, 0))
                        else:
                            xp = fb[t, k + 1, pl.ds(i * ROWS + 1, ROWS), :]
                        yp = pltpu.roll(jnp.where(low, fb[t, k + 2, rows, :], f), LANES - NZ, 1)
                        ym = pltpu.roll(jnp.where(high, fb[t, k, rows, :], f), NZ, 1)
                        zp = pltpu.roll(jnp.where(at_first, 0.0, f), LANES - 1, 1)
                        zm = pltpu.roll(jnp.where(at_last, 0.0, f), 1, 1)
                        near = (xm + xp) + (yp + ym) + (zp + zm)
                        g = f * (linear + f * (0.25 * f - 0.9)) - near
                        gb[t, k, rows, :] = g
                        gs.append(g)
                    before, after = gs[0], gs[-1]
                    for t in range(1, slices):
                        before = r * before + gs[t]
                        after = r * after + gs[slices - 1 - t]
                    mom[it, part, half, k, 0] = before
                    mom[it, part, half, k, 1] = after

    def solve(it, part):
        @pl.loop(0, tiles // 4)
        def _(quad):
            for j in range(4):
                k = quad * 4 + j
                for half, i in enumerate(parts[part]):
                    rows = pl.ds(i * ROWS, ROWS)
                    gs = [gb[t, k, rows, :] for t in range(slices)]
                    state = yv[it, part, half, k, 0]
                    states = []
                    for t in range(slices):
                        state = r * state + gs[t]
                        states.append(state)
                    ahead = r * yv[it, part, half, k, 1]
                    for t in reversed(range(slices)):
                        new = keep * fb[t, k + 1, rows, :] - gain * (states[t] + ahead)
                        if it + 1 < ITERS:
                            fb[t, k + 1, rows, :] = new
                        else:
                            out[t, rows, pl.ds(pl.multiple_of(k * LANES, LANES), LANES)] = new
                        if it + 1 < ITERS and i == 0:
                            hs[it + 1, 1, t, pl.ds(k, 1), :] = new[:1]
                        if it + 1 < ITERS and i == groups - 1:
                            hs[it + 1, 0, t, pl.ds(k, 1), :] = new[ROWS - 1 :]
                        ahead = r * (gs[t] + ahead)

    pending = []

    def copy(src, dst, send_sem, recv_sem, device):
        return pltpu.make_async_remote_copy(
            src_ref=src, dst_ref=dst, send_sem=send_sem, recv_sem=recv_sem, device_id=device, device_id_type=MESH
        )

    def start(src, dst, it, part, a, b, device):
        one_copy = copy(src, dst, send.at[it, part, a], recv.at[it, part, b], device)
        one_copy.start()
        pending.append(one_copy)

    def arrive(dst, it, part, b):
        copy(dst, dst, send.at[it, part, b], recv.at[it, part, b], other).wait_recv()

    def pack(it):
        @pl.loop(0, slices)
        def _(t):
            for which, edge in enumerate((groups * ROWS - 1, 0)):
                for k in range(tiles):
                    hs[it, which, t, pl.ds(k, 1), :] = fb[t, k + 1, pl.ds(edge, 1), :]

    def halo(it, which):
        return copy(
            hs.at[it, which],
            hb.at[it, which],
            hsend.at[it, which],
            hrecv.at[it, which],
            (tm, sp + 1) if which == 0 else (tm, sp - 1),
        )

    def send_halo(it):
        pl.when(has_right)(lambda: halo(it, 0).start())
        pl.when(has_left)(lambda: halo(it, 1).start())

    def wait_halo(it):
        pl.when(has_left)(lambda: halo(it, 0).wait_recv())
        pl.when(has_right)(lambda: halo(it, 1).wait_recv())

    up = lambda d, hd: 1 + 2 * d + hd
    down = lambda d, hd: 1 + 2 * nz + 2 * d + hd
    back = 1 + 4 * nz

    def up_core(it, part):
        start(mom.at[it, part, 1 - c], u1.at[it, part], it, part, 0, 0, other)

    def up_owner(it, part):
        arrive(u1.at[it, part], it, part, 0)
        for k in range(tiles):
            xs[it, part, k, 0] = wa * mom[it, part, c, k, 0] + wb * u1[it, part, k, 0]
            xs[it, part, k, 1] = wb * mom[it, part, c, k, 1] + wa * u1[it, part, k, 1]
        for d in far_first:
            for hd in range(2):
                src = xs.at[it, part, hd * nz + (z + d) % nz]
                start(src, zr.at[it, part, z * 2 + h], it, part, up(d, hd), up(d, h), owner(d, hd))

    def down_owner(it, part):
        for d in reversed(far_first):
            for hd in range(2):
                arrive(zr.at[it, part, ((z + nz - d) % nz) * 2 + hd], it, part, up(d, hd))
        ms = [zr[it, part, j, 0] for j in range(2 * nz)]
        ns = [zr[it, part, j, 1] for j in range(2 * nz)]
        left, right, ratio = ms, ns, r16
        while len(left) > 1:
            pairs = range(0, len(left), 2)
            left = [ratio * left[j] + left[j + 1] for j in pairs]
            right = [right[j] + ratio * right[j + 1] for j in pairs]
            ratio = ratio * ratio
        before, after = inv * left[0], inv * right[0]
        for j in range(2 * nz):
            ws[it, part, j, 0] = before
            ws[it, part, 2 * nz - 1 - j, 1] = after
            before = r16 * before + ms[j]
            after = r16 * after + ns[2 * nz - 1 - j]
        for d in far_first:
            for hd in range(2):
                src = ws.at[it, part, ((z + d) % nz) * 2 + hd]
                start(src, wr.at[it, part, h * nz + z], it, part, down(d, hd), down(d, h), owner(d, hd))

    def down_core(it, part):
        for d in reversed(far_first):
            for hd in range(2):
                arrive(wr.at[it, part, hd * nz + (z + nz - d) % nz], it, part, down(d, hd))
        for k in range(tiles):
            before, after = wr[it, part, k, 0], wr[it, part, k, 1]
            cs[it, part, k, 0] = wa * before + za * mom[it, part, c, k, 0]
            cs[it, part, k, 1] = wb * after + zb * mom[it, part, c, k, 1]
        start(cs.at[it, part], yv.at[it, part, c], it, part, back, back, other)
        for k in range(tiles):
            before, after = wr[it, part, k, 0], wr[it, part, k, 1]
            yv[it, part, c, k, 0] = wb * before + zb * u1[it, part, k, 0]
            yv[it, part, c, k, 1] = wa * after + za * u1[it, part, k, 1]

    for load in loads:
        load.wait()
    pack(0)
    stencil(0, 0)
    pl.semaphore_wait(barrier, 2 * nz + 1 + has_left.astype(jnp.int32) + has_right.astype(jnp.int32))
    send_halo(0)
    for it in range(ITERS):
        up_core(it, 0)
        up_owner(it, 0)
        wait_halo(it)
        stencil(it, 1)
        up_core(it, 1)
        up_owner(it, 1)
        for phase in (down_owner, down_core):
            for part in range(2):
                phase(it, part)
        for part in range(2):
            arrive(yv.at[it, part, 1 - c], it, part, back)
            solve(it, part)
        if it + 1 < ITERS:
            send_halo(it + 1)
            stencil(it + 1, 0)
    for one_copy in pending:
        one_copy.wait_send()
    for it in range(ITERS):
        pl.when(has_right)(lambda: halo(it, 0).wait_send())
        pl.when(has_left)(lambda: halo(it, 1).wait_send())


def solution(mesh):
    nz = mesh.shape["tm"] // 4
    ny = mesh.shape["space"] // 2

    def on_device(field, step, mass):
        slices, planes, width = field.shape
        tiles = width // LANES
        tile = (ROWS, LANES)
        vmem = lambda *shape: pltpu.VMEM(shape, jnp.float32)
        level = (ITERS, 2)
        sems = 2 + 4 * nz
        return pl.pallas_call(
            functools.partial(kernel, nz, ny, slices),
            out_shape=jax.ShapeDtypeStruct(field.shape, field.dtype),
            in_specs=[
                pl.BlockSpec(memory_space=pltpu.SMEM),
                pl.BlockSpec(memory_space=pltpu.SMEM),
                pl.BlockSpec(memory_space=pltpu.HBM),
            ],
            out_specs=pl.BlockSpec(memory_space=pltpu.VMEM),
            scratch_shapes=[
                vmem(slices, tiles + 2, planes, LANES),
                vmem(slices, tiles, planes, LANES),
                vmem(ITERS, 2, slices, tiles, LANES),
                vmem(ITERS, 2, slices, tiles, LANES),
                vmem(*level, 2, tiles, 2, *tile),
                vmem(*level, tiles, 2, *tile),
                vmem(*level, tiles, 2, *tile),
                vmem(*level, tiles, 2, *tile),
                vmem(*level, tiles, 2, *tile),
                vmem(*level, tiles, 2, *tile),
                vmem(*level, tiles, 2, *tile),
                vmem(*level, 2, tiles, 2, *tile),
                pltpu.SemaphoreType.DMA((tiles,)),
                pltpu.SemaphoreType.DMA((*level, sems)),
                pltpu.SemaphoreType.DMA((*level, sems)),
                pltpu.SemaphoreType.DMA((ITERS, 2)),
                pltpu.SemaphoreType.DMA((ITERS, 2)),
            ],
            compiler_params=pltpu.CompilerParams(
                collective_id=0, has_side_effects=True, vmem_limit_bytes=VMEM_MIB * 1024 * 1024
            ),
        )(step, mass, pltpu.with_memory_space_constraint(field, pltpu.HBM))

    return jax.shard_map(
        on_device,
        mesh=mesh,
        in_specs=(P("tm", "space", None), P(), P()),
        out_specs=P("tm", "space", None),
        check_vma=False,
    )
```

```python
import functools

import jax
import jax.numpy as jnp
from jax import lax
from jax.experimental import pallas as pl
from jax.experimental.pallas import tpu as pltpu
from jax.sharding import PartitionSpec as P

NZ = 32
ITERS = 2
VMEM_MIB = 40
LANES = 128
ROWS = 8
MESH = pl.DeviceIdType.MESH


def kernel(nz, ny, slices, step_ref, mass_ref, field, out, fb, gb, hs, hb, hm, mom, u1, xs, zr, ws, wr, cs, yv,
           load_sem, send, recv, hsend, hrecv):
    tiles = fb.shape[1] - 2
    groups = fb.shape[2] // ROWS - 2
    tm, sp = lax.axis_index("tm"), lax.axis_index("space")
    z, h, c = tm // 4, (tm // 2) % 2, tm % 2
    lo, y = sp // ny, sp % ny
    last = 2 * ny - 1
    other = (tm + 1 - 2 * c, sp)
    owner = lambda d, hd: (((z + d) % nz) * 4 + hd * 2 + c, (1 - lo) * ny + y)
    has_left, has_right = sp > 0, sp < last

    barrier = pltpu.get_barrier_semaphore()

    def greet(device):
        pl.semaphore_signal(barrier, inc=1, device_id=device, device_id_type=MESH)

    far_first = sorted(range(nz), key=lambda d: (-min(d, nz - d), d))
    for d in far_first:
        for hd in range(2):
            greet(owner(d, hd))
    greet(other)

    @pl.when(has_left)
    def _():
        greet((tm, sp - 1))

    @pl.when(has_right)
    def _():
        greet((tm, sp + 1))

    loads = [
        pltpu.make_async_copy(
            field.at[:, :, pl.ds(k * LANES, LANES)],
            fb.at[:, k + 1, pl.ds(ROWS, groups * ROWS), :],
            load_sem.at[k],
        )
        for k in range(tiles)
    ]
    for load in loads:
        load.start()

    full = lambda value: jnp.full((ROWS, LANES), value, jnp.float32)
    blank = full(0.0)

    @pl.loop(0, slices)
    def _(t):
        for k in (0, tiles + 1):
            for i in range(groups):
                fb[t, k, pl.ds((i + 1) * ROWS, ROWS), :] = blank
        for k in range(tiles):
            fb[t, k + 1, pl.ds(0, ROWS), :] = blank
            fb[t, k + 1, pl.ds((groups + 1) * ROWS, ROWS), :] = blank

    def clear(which):
        for it in range(ITERS):
            hb[it, which] = jnp.zeros(hb.shape[2:], jnp.float32)

    pl.when(jnp.logical_not(has_left))(lambda: clear(0))
    pl.when(jnp.logical_not(has_right))(lambda: clear(1))

    m = full(mass_ref[0])
    s = full(step_ref[0])
    m2 = m * m
    q = m * jnp.sqrt(1.0 + 0.25 * m2) - 0.5 * m2
    double = lambda p: p * (2.0 - p)
    r = 1.0 - q
    q8 = double(double(double(q)))
    q16 = double(q8)
    r8, r16 = 1.0 - q8, 1.0 - q16
    whole = q16
    for _ in range((2 * nz - 1).bit_length()):
        whole = double(whole)
    inv = 1.0 / whole
    linear = 7.0 - m2
    keep = 1.0 - s
    gain = s * r / (q * (1.0 + r))
    first = c == 0
    one = full(1.0)
    wa, wb = jnp.where(first, r8, one), jnp.where(first, one, r8)
    za, zb = jnp.where(first, one, blank), jnp.where(first, blank, one)

    lane = lax.broadcasted_iota(jnp.int32, (ROWS, LANES), 1)
    row = lax.broadcasted_iota(jnp.int32, (ROWS, LANES), 0)
    zplace = lane % NZ
    at_first, at_last = zplace == 0, zplace == NZ - 1
    low, high = lane < NZ, lane >= LANES - NZ
    top, bottom = row == 0, row == ROWS - 1

    parts = (tuple(range(1, groups - 1)), (0, groups - 1))

    def stencil(it, part, lacks):
        @pl.loop(0, tiles // 4)
        def _(quad):
            for k in (quad * 4 + j for j in range(4)):
                for half, i in enumerate(parts[part]):
                    rows = pl.ds((i + 1) * ROWS, ROWS)
                    gs = []
                    for t in range(slices):
                        f = fb[t, k + 1, rows, :]
                        xm = fb[t, k + 1, pl.ds((i + 1) * ROWS - 1, ROWS), :]
                        xp = fb[t, k + 1, pl.ds((i + 1) * ROWS + 1, ROWS), :]
                        if lacks and half == 0:
                            xm = jnp.where(top, 0.0, xm)
                        if lacks and half == 1:
                            xp = jnp.where(bottom, 0.0, xp)
                        yp = pltpu.roll(jnp.where(low, fb[t, k + 2, rows, :], f), LANES - NZ, 1)
                        ym = pltpu.roll(jnp.where(high, fb[t, k, rows, :], f), NZ, 1)
                        zp = pltpu.roll(jnp.where(at_first, 0.0, f), LANES - 1, 1)
                        zm = pltpu.roll(jnp.where(at_last, 0.0, f), 1, 1)
                        near = (xm + xp) + (yp + ym) + (zp + zm)
                        g = f * (linear + f * (0.25 * f - 0.9)) - near
                        gb[t, k, pl.ds(i * ROWS, ROWS), :] = g
                        gs.append(g)
                    before, after = gs[0], gs[-1]
                    for t in range(1, slices):
                        before = r * before + gs[t]
                        after = r * after + gs[slices - 1 - t]
                    mom[it, part, half, k, 0] = before
                    mom[it, part, half, k, 1] = after

    edges = (top, bottom)

    def mend_outer_sums(it):
        for half in range(2):
            for lo_k in range(0, tiles, ROWS):
                band = pl.ds(lo_k, ROWS)
                planes = [hb[it, half, t, band, :] for t in range(slices)]
                before, after = planes[0], planes[-1]
                for t in range(1, slices):
                    before = r * before + planes[t]
                    after = r * after + planes[slices - 1 - t]
                hm[half, 0, band, :] = before
                hm[half, 1, band, :] = after
            for k in range(tiles):
                for which in range(2):
                    add = jnp.where(edges[half], hm[half, which, pl.ds(k, 1), :], 0.0)
                    mom[it, 1, half, k, which] = mom[it, 1, half, k, which] - add

    def mend_outer(it):
        @pl.loop(0, slices)
        def _(t):
            for half, i in enumerate(parts[1]):
                rows = pl.ds(i * ROWS, ROWS)
                for k in range(tiles):
                    add = jnp.where(edges[half], hb[it, half, t, pl.ds(k, 1), :], 0.0)
                    gb[t, k, rows, :] = gb[t, k, rows, :] - add

    def mend_inner(it):
        @pl.loop(0, slices)
        def _(t):
            for half, i in enumerate(parts[0]):
                rows = pl.ds(i * ROWS, ROWS)
                for k in range(tiles):
                    shifted = fb[t, k + 1, pl.ds((i + 1) * ROWS + 2 * half - 1, ROWS), :]
                    gb[t, k, rows, :] = gb[t, k, rows, :] - jnp.where(edges[half], shifted, 0.0)

    def solve(it, part):
        @pl.loop(0, tiles // 4)
        def _(quad):
            for j in range(4):
                k = quad * 4 + j
                for half, i in enumerate(parts[part]):
                    rows = pl.ds((i + 1) * ROWS, ROWS)
                    gs = [gb[t, k, pl.ds(i * ROWS, ROWS), :] for t in range(slices)]
                    state = yv[it, part, half, k, 0]
                    states = []
                    for t in range(slices):
                        state = r * state + gs[t]
                        states.append(state)
                    ahead = r * yv[it, part, half, k, 1]
                    news = [None] * slices
                    for t in reversed(range(slices)):
                        new = keep * fb[t, k + 1, rows, :] - gain * (states[t] + ahead)
                        ahead = r * (gs[t] + ahead)
                        news[t] = new
                        if it + 1 < ITERS:
                            fb[t, k + 1, rows, :] = new
                        else:
                            out[t, pl.ds(i * ROWS, ROWS), pl.ds(pl.multiple_of(k * LANES, LANES), LANES)] = new
                        if it + 1 < ITERS and part == 1:
                            edge = half * (ROWS - 1)
                            hs[it + 1, 1 - half, t, pl.ds(k, 1), :] = new[edge : edge + 1]
                    if it + 1 < ITERS and part == 1:
                        before, after = news[0], news[-1]
                        for t in range(1, slices):
                            before = r * before + news[t]
                            after = r * after + news[slices - 1 - t]
                        turn = (1, ROWS - 1)[half]
                        for which, add in enumerate((before, after)):
                            add = jnp.where(edges[half], pltpu.roll(add, turn, 0), 0.0)
                            mom[it + 1, 0, half, k, which] = mom[it + 1, 0, half, k, which] - add

    pending = []

    def copy(src, dst, send_sem, recv_sem, device):
        return pltpu.make_async_remote_copy(
            src_ref=src, dst_ref=dst, send_sem=send_sem, recv_sem=recv_sem, device_id=device, device_id_type=MESH
        )

    def start(src, dst, it, part, a, b, device):
        one_copy = copy(src, dst, send.at[it, part, a], recv.at[it, part, b], device)
        one_copy.start()
        pending.append(one_copy)

    def arrive(dst, it, part, b):
        copy(dst, dst, send.at[it, part, b], recv.at[it, part, b], other).wait_recv()

    def pack(it):
        @pl.loop(0, slices)
        def _(t):
            for which, edge in enumerate((groups * ROWS - 1, 0)):
                for k in range(tiles):
                    hs[it, which, t, pl.ds(k, 1), :] = fb[t, k + 1, pl.ds(ROWS + edge, 1), :]

    def halo(it, which):
        return copy(
            hs.at[it, which],
            hb.at[it, which],
            hsend.at[it, which],
            hrecv.at[it, which],
            (tm, sp + 1) if which == 0 else (tm, sp - 1),
        )

    def send_halo(it):
        pl.when(has_right)(lambda: halo(it, 0).start())
        pl.when(has_left)(lambda: halo(it, 1).start())

    def wait_halo(it):
        pl.when(has_left)(lambda: halo(it, 0).wait_recv())
        pl.when(has_right)(lambda: halo(it, 1).wait_recv())

    up = lambda d, hd: 1 + 2 * d + hd
    down = lambda d, hd: 1 + 2 * nz + 2 * d + hd
    back = 1 + 4 * nz

    def up_core(it, part):
        start(mom.at[it, part, 1 - c], u1.at[it, part], it, part, 0, 0, other)

    def up_owner(it, part):
        arrive(u1.at[it, part], it, part, 0)
        for k in range(tiles):
            xs[it, part, k, 0] = wa * mom[it, part, c, k, 0] + wb * u1[it, part, k, 0]
            xs[it, part, k, 1] = wb * mom[it, part, c, k, 1] + wa * u1[it, part, k, 1]
        for d in far_first:
            for hd in range(2):
                src = xs.at[it, part, hd * nz + (z + d) % nz]
                start(src, zr.at[it, part, z * 2 + h], it, part, up(d, hd), up(d, h), owner(d, hd))

    def down_owner(it, part):
        for d in reversed(far_first):
            for hd in range(2):
                arrive(zr.at[it, part, ((z + nz - d) % nz) * 2 + hd], it, part, up(d, hd))
        ms = [zr[it, part, j, 0] for j in range(2 * nz)]
        ns = [zr[it, part, j, 1] for j in range(2 * nz)]
        left, right, ratio = ms, ns, r16
        while len(left) > 1:
            pairs = range(0, len(left), 2)
            left = [ratio * left[j] + left[j + 1] for j in pairs]
            right = [right[j] + ratio * right[j + 1] for j in pairs]
            ratio = ratio * ratio
        before, after = inv * left[0], inv * right[0]
        for j in range(2 * nz):
            ws[it, part, j, 0] = before
            ws[it, part, 2 * nz - 1 - j, 1] = after
            before = r16 * before + ms[j]
            after = r16 * after + ns[2 * nz - 1 - j]
        for d in far_first:
            for hd in range(2):
                src = ws.at[it, part, ((z + d) % nz) * 2 + hd]
                start(src, wr.at[it, part, h * nz + z], it, part, down(d, hd), down(d, h), owner(d, hd))

    def down_core(it, part):
        for d in reversed(far_first):
            for hd in range(2):
                arrive(wr.at[it, part, hd * nz + (z + nz - d) % nz], it, part, down(d, hd))
        for k in range(tiles):
            before, after = wr[it, part, k, 0], wr[it, part, k, 1]
            cs[it, part, k, 0] = wa * before + za * mom[it, part, c, k, 0]
            cs[it, part, k, 1] = wb * after + zb * mom[it, part, c, k, 1]
        start(cs.at[it, part], yv.at[it, part, c], it, part, back, back, other)
        for k in range(tiles):
            before, after = wr[it, part, k, 0], wr[it, part, k, 1]
            yv[it, part, c, k, 0] = wb * before + zb * u1[it, part, k, 0]
            yv[it, part, c, k, 1] = wa * after + za * u1[it, part, k, 1]

    for load in loads:
        load.wait()
    pack(0)
    stencil(0, 0, False)
    pl.semaphore_wait(barrier, 2 * nz + 1 + has_left.astype(jnp.int32) + has_right.astype(jnp.int32))
    send_halo(0)
    for it in range(ITERS):
        up_core(it, 0)
        stencil(it, 1, False)
        up_owner(it, 0)
        wait_halo(it)
        mend_outer_sums(it)
        up_core(it, 1)
        mend_outer(it)
        if it > 0:
            mend_inner(it)
        up_owner(it, 1)
        for phase in (down_owner, down_core):
            for part in range(2):
                phase(it, part)
        arrive(yv.at[it, 0, 1 - c], it, 0, back)
        solve(it, 0)
        if it + 1 < ITERS:
            stencil(it + 1, 0, True)
        arrive(yv.at[it, 1, 1 - c], it, 1, back)
        solve(it, 1)
        if it + 1 < ITERS:
            send_halo(it + 1)
    for one_copy in pending:
        one_copy.wait_send()
    for it in range(ITERS):
        pl.when(has_right)(lambda: halo(it, 0).wait_send())
        pl.when(has_left)(lambda: halo(it, 1).wait_send())


def solution(mesh):
    nz = mesh.shape["tm"] // 4
    ny = mesh.shape["space"] // 2

    def on_device(field, step, mass):
        slices, planes, width = field.shape
        tiles = width // LANES
        tile = (ROWS, LANES)
        vmem = lambda *shape: pltpu.VMEM(shape, jnp.float32)
        level = (ITERS, 2)
        sems = 2 + 4 * nz
        return pl.pallas_call(
            functools.partial(kernel, nz, ny, slices),
            out_shape=jax.ShapeDtypeStruct(field.shape, field.dtype),
            in_specs=[
                pl.BlockSpec(memory_space=pltpu.SMEM),
                pl.BlockSpec(memory_space=pltpu.SMEM),
                pl.BlockSpec(memory_space=pltpu.HBM),
            ],
            out_specs=pl.BlockSpec(memory_space=pltpu.VMEM),
            scratch_shapes=[
                vmem(slices, tiles + 2, planes + 2 * ROWS, LANES),
                vmem(slices, tiles, planes, LANES),
                vmem(ITERS, 2, slices, tiles, LANES),
                vmem(ITERS, 2, slices, tiles, LANES),
                vmem(2, 2, tiles, LANES),
                vmem(*level, 2, tiles, 2, *tile),
                vmem(*level, tiles, 2, *tile),
                vmem(*level, tiles, 2, *tile),
                vmem(*level, tiles, 2, *tile),
                vmem(*level, tiles, 2, *tile),
                vmem(*level, tiles, 2, *tile),
                vmem(*level, tiles, 2, *tile),
                vmem(*level, 2, tiles, 2, *tile),
                pltpu.SemaphoreType.DMA((tiles,)),
                pltpu.SemaphoreType.DMA((*level, sems)),
                pltpu.SemaphoreType.DMA((*level, sems)),
                pltpu.SemaphoreType.DMA((ITERS, 2)),
                pltpu.SemaphoreType.DMA((ITERS, 2)),
            ],
            compiler_params=pltpu.CompilerParams(
                collective_id=0, has_side_effects=True, vmem_limit_bytes=VMEM_MIB * 1024 * 1024
            ),
        )(step, mass, pltpu.with_memory_space_constraint(field, pltpu.HBM))

    return jax.shard_map(
        on_device,
        mesh=mesh,
        in_specs=(P("tm", "space", None), P(), P()),
        out_specs=P("tm", "space", None),
        check_vma=False,
    )
```

```python
import functools

import jax
import jax.numpy as jnp
from jax import lax
from jax.experimental import pallas as pl
from jax.experimental.pallas import tpu as pltpu
from jax.sharding import PartitionSpec as P

NZ = 32
ITERS = 2
VMEM_MIB = 40
LANES = 128
ROWS = 8
MESH = pl.DeviceIdType.MESH


def kernel(nz, ny, slices, step_ref, mass_ref, field, out, fb, gb, hs, hb, hq, hm, mom, u1, xs, zr, ws, wr, cs, yv,
           load_sem, send, recv, hsend, hrecv):
    tiles = fb.shape[1] - 2
    groups = fb.shape[2] // ROWS - 2
    tm, sp = lax.axis_index("tm"), lax.axis_index("space")
    z, h, c = tm // 4, (tm // 2) % 2, tm % 2
    lo, y = sp // ny, sp % ny
    last = 2 * ny - 1
    other = (tm + 1 - 2 * c, sp)
    owner = lambda d, hd: (((z + d) % nz) * 4 + hd * 2 + c, (1 - lo) * ny + y)
    has_left, has_right = sp > 0, sp < last

    barrier = pltpu.get_barrier_semaphore()

    def greet(device):
        pl.semaphore_signal(barrier, inc=1, device_id=device, device_id_type=MESH)

    far_first = sorted(range(nz), key=lambda d: (-min(d, nz - d), d))
    for d in far_first:
        for hd in range(2):
            greet(owner(d, hd))
    greet(other)

    @pl.when(has_left)
    def _():
        greet((tm, sp - 1))

    @pl.when(has_right)
    def _():
        greet((tm, sp + 1))

    loads = [
        pltpu.make_async_copy(
            field.at[:, :, pl.ds(k * LANES, LANES)],
            fb.at[:, k + 1, pl.ds(ROWS, groups * ROWS), :],
            load_sem.at[k],
        )
        for k in range(tiles)
    ]
    for load in loads:
        load.start()

    full = lambda value: jnp.full((ROWS, LANES), value, jnp.float32)
    blank = full(0.0)

    @pl.loop(0, slices)
    def _(t):
        for k in (0, tiles + 1):
            for i in range(groups):
                fb[t, k, pl.ds((i + 1) * ROWS, ROWS), :] = blank
        for k in range(tiles):
            fb[t, k + 1, pl.ds(0, ROWS), :] = blank
            fb[t, k + 1, pl.ds((groups + 1) * ROWS, ROWS), :] = blank

    def clear(which):
        for it in range(ITERS):
            hb[it, which] = jnp.zeros(hb.shape[2:], jnp.float32)
            hm[it, which] = jnp.zeros(hm.shape[2:], jnp.float32)

    pl.when(jnp.logical_not(has_left))(lambda: clear(0))
    pl.when(jnp.logical_not(has_right))(lambda: clear(1))

    m = full(mass_ref[0])
    s = full(step_ref[0])
    m2 = m * m
    q = m * jnp.sqrt(1.0 + 0.25 * m2) - 0.5 * m2
    double = lambda p: p * (2.0 - p)
    r = 1.0 - q
    q8 = double(double(double(q)))
    q16 = double(q8)
    r8, r16 = 1.0 - q8, 1.0 - q16
    whole = q16
    for _ in range((2 * nz - 1).bit_length()):
        whole = double(whole)
    inv = 1.0 / whole
    linear = 7.0 - m2
    keep = 1.0 - s
    gain = s * r / (q * (1.0 + r))
    first = c == 0
    one = full(1.0)
    wa, wb = jnp.where(first, r8, one), jnp.where(first, one, r8)
    za, zb = jnp.where(first, one, blank), jnp.where(first, blank, one)

    lane = lax.broadcasted_iota(jnp.int32, (ROWS, LANES), 1)
    row = lax.broadcasted_iota(jnp.int32, (ROWS, LANES), 0)
    zplace = lane % NZ
    at_first, at_last = zplace == 0, zplace == NZ - 1
    low, high = lane < NZ, lane >= LANES - NZ
    top, bottom = row == 0, row == ROWS - 1

    parts = (tuple(range(1, groups - 1)), (0, groups - 1))

    def stencil(it, part, lacks):
        @pl.loop(0, tiles // 4)
        def _(quad):
            for k in (quad * 4 + j for j in range(4)):
                for half, i in enumerate(parts[part]):
                    rows = pl.ds((i + 1) * ROWS, ROWS)
                    gs = []
                    for t in range(slices):
                        f = fb[t, k + 1, rows, :]
                        xm = fb[t, k + 1, pl.ds((i + 1) * ROWS - 1, ROWS), :]
                        xp = fb[t, k + 1, pl.ds((i + 1) * ROWS + 1, ROWS), :]
                        if lacks and half == 0:
                            xm = jnp.where(top, 0.0, xm)
                        if lacks and half == 1:
                            xp = jnp.where(bottom, 0.0, xp)
                        yp = pltpu.roll(jnp.where(low, fb[t, k + 2, rows, :], f), LANES - NZ, 1)
                        ym = pltpu.roll(jnp.where(high, fb[t, k, rows, :], f), NZ, 1)
                        zp = pltpu.roll(jnp.where(at_first, 0.0, f), LANES - 1, 1)
                        zm = pltpu.roll(jnp.where(at_last, 0.0, f), 1, 1)
                        near = (xm + xp) + (yp + ym) + (zp + zm)
                        g = f * (linear + f * (0.25 * f - 0.9)) - near
                        gb[t, k, pl.ds(i * ROWS, ROWS), :] = g
                        gs.append(g)
                    before, after = gs[0], gs[-1]
                    for t in range(1, slices):
                        before = r * before + gs[t]
                        after = r * after + gs[slices - 1 - t]
                    mom[it, part, half, k, 0] = before
                    mom[it, part, half, k, 1] = after

    edges = (top, bottom)

    def edge_sums(it):
        for side in range(2):
            for lo_k in range(0, tiles, ROWS):
                band = pl.ds(lo_k, ROWS)
                planes = [hs[it, side, t, band, :] for t in range(slices)]
                before, after = planes[0], planes[-1]
                for t in range(1, slices):
                    before = r * before + planes[t]
                    after = r * after + planes[slices - 1 - t]
                hq[it, side, 0, band, :] = before
                hq[it, side, 1, band, :] = after

    def mend_outer_sums(it):
        for half in range(2):
            for k in range(tiles):
                for which in range(2):
                    add = jnp.where(edges[half], hm[it, half, which, pl.ds(k, 1), :], 0.0)
                    mom[it, 1, half, k, which] = mom[it, 1, half, k, which] - add

    def mend_outer(it):
        @pl.loop(0, slices)
        def _(t):
            for half, i in enumerate(parts[1]):
                rows = pl.ds(i * ROWS, ROWS)
                for k in range(tiles):
                    add = jnp.where(edges[half], hb[it, half, t, pl.ds(k, 1), :], 0.0)
                    gb[t, k, rows, :] = gb[t, k, rows, :] - add

    def mend_inner(it):
        @pl.loop(0, slices)
        def _(t):
            for half, i in enumerate(parts[0]):
                rows = pl.ds(i * ROWS, ROWS)
                for k in range(tiles):
                    shifted = fb[t, k + 1, pl.ds((i + 1) * ROWS + 2 * half - 1, ROWS), :]
                    gb[t, k, rows, :] = gb[t, k, rows, :] - jnp.where(edges[half], shifted, 0.0)

    def solve(it, part, halves):
        @pl.loop(0, tiles // 4)
        def _(quad):
            for j in range(4):
                k = quad * 4 + j
                for half in halves:
                    i = parts[part][half]
                    rows = pl.ds((i + 1) * ROWS, ROWS)
                    gs = [gb[t, k, pl.ds(i * ROWS, ROWS), :] for t in range(slices)]
                    state = yv[it, part, half, k, 0]
                    states = []
                    for t in range(slices):
                        state = r * state + gs[t]
                        states.append(state)
                    ahead = r * yv[it, part, half, k, 1]
                    news = [None] * slices
                    for t in reversed(range(slices)):
                        new = keep * fb[t, k + 1, rows, :] - gain * (states[t] + ahead)
                        ahead = r * (gs[t] + ahead)
                        news[t] = new
                        if it + 1 < ITERS:
                            fb[t, k + 1, rows, :] = new
                        else:
                            out[t, pl.ds(i * ROWS, ROWS), pl.ds(pl.multiple_of(k * LANES, LANES), LANES)] = new
                        if it + 1 < ITERS and part == 1:
                            edge = half * (ROWS - 1)
                            hs[it + 1, 1 - half, t, pl.ds(k, 1), :] = new[edge : edge + 1]
                    if it + 1 < ITERS and part == 1:
                        before, after = news[0], news[-1]
                        for t in range(1, slices):
                            before = r * before + news[t]
                            after = r * after + news[slices - 1 - t]
                        turn, at = (1, ROWS - 1)[half], half * (ROWS - 1)
                        for which, add in enumerate((before, after)):
                            hq[it + 1, 1 - half, which, pl.ds(k, 1), :] = add[at : at + 1]
                            add = jnp.where(edges[half], pltpu.roll(add, turn, 0), 0.0)
                            mom[it + 1, 0, half, k, which] = mom[it + 1, 0, half, k, which] - add

    pending = []

    def copy(src, dst, send_sem, recv_sem, device):
        return pltpu.make_async_remote_copy(
            src_ref=src, dst_ref=dst, send_sem=send_sem, recv_sem=recv_sem, device_id=device, device_id_type=MESH
        )

    def start(src, dst, it, part, a, b, device):
        one_copy = copy(src, dst, send.at[it, part, a], recv.at[it, part, b], device)
        one_copy.start()
        pending.append(one_copy)

    def arrive(dst, it, part, b):
        copy(dst, dst, send.at[it, part, b], recv.at[it, part, b], other).wait_recv()

    def pack(it):
        @pl.loop(0, slices)
        def _(t):
            for which, edge in enumerate((groups * ROWS - 1, 0)):
                for k in range(tiles):
                    hs[it, which, t, pl.ds(k, 1), :] = fb[t, k + 1, pl.ds(ROWS + edge, 1), :]

    def halo(it, which, kind):
        src, dst = ((hq, hm), (hs, hb))[kind]
        return copy(
            src.at[it, which],
            dst.at[it, which],
            hsend.at[it, which, kind],
            hrecv.at[it, which, kind],
            (tm, sp + 1) if which == 0 else (tm, sp - 1),
        )

    def send_halo(it, kind):
        pl.when(has_right)(lambda: halo(it, 0, kind).start())
        pl.when(has_left)(lambda: halo(it, 1, kind).start())

    def wait_halo(it, kind):
        pl.when(has_left)(lambda: halo(it, 0, kind).wait_recv())
        pl.when(has_right)(lambda: halo(it, 1, kind).wait_recv())

    up = lambda d, hd: 1 + 2 * d + hd
    down = lambda d, hd: 1 + 2 * nz + 2 * d + hd
    back = 1 + 4 * nz

    def up_core(it, part):
        start(mom.at[it, part, 1 - c], u1.at[it, part], it, part, 0, 0, other)

    def up_owner(it, part):
        arrive(u1.at[it, part], it, part, 0)
        for k in range(tiles):
            xs[it, part, k, 0] = wa * mom[it, part, c, k, 0] + wb * u1[it, part, k, 0]
            xs[it, part, k, 1] = wb * mom[it, part, c, k, 1] + wa * u1[it, part, k, 1]
        for d in far_first:
            for hd in range(2):
                src = xs.at[it, part, hd * nz + (z + d) % nz]
                start(src, zr.at[it, part, z * 2 + h], it, part, up(d, hd), up(d, h), owner(d, hd))

    def down_owner(it, part):
        for d in reversed(far_first):
            for hd in range(2):
                arrive(zr.at[it, part, ((z + nz - d) % nz) * 2 + hd], it, part, up(d, hd))
        ms = [zr[it, part, j, 0] for j in range(2 * nz)]
        ns = [zr[it, part, j, 1] for j in range(2 * nz)]
        left, right, ratio = ms, ns, r16
        while len(left) > 1:
            pairs = range(0, len(left), 2)
            left = [ratio * left[j] + left[j + 1] for j in pairs]
            right = [right[j] + ratio * right[j + 1] for j in pairs]
            ratio = ratio * ratio
        before, after = inv * left[0], inv * right[0]
        for j in range(2 * nz):
            ws[it, part, j, 0] = before
            ws[it, part, 2 * nz - 1 - j, 1] = after
            before = r16 * before + ms[j]
            after = r16 * after + ns[2 * nz - 1 - j]
        for d in far_first:
            for hd in range(2):
                src = ws.at[it, part, ((z + d) % nz) * 2 + hd]
                start(src, wr.at[it, part, h * nz + z], it, part, down(d, hd), down(d, h), owner(d, hd))

    def down_core(it, part):
        for d in reversed(far_first):
            for hd in range(2):
                arrive(wr.at[it, part, hd * nz + (z + nz - d) % nz], it, part, down(d, hd))
        for k in range(tiles):
            before, after = wr[it, part, k, 0], wr[it, part, k, 1]
            cs[it, part, k, 0] = wa * before + za * mom[it, part, c, k, 0]
            cs[it, part, k, 1] = wb * after + zb * mom[it, part, c, k, 1]
        start(cs.at[it, part], yv.at[it, part, c], it, part, back, back, other)
        for k in range(tiles):
            before, after = wr[it, part, k, 0], wr[it, part, k, 1]
            yv[it, part, c, k, 0] = wb * before + zb * u1[it, part, k, 0]
            yv[it, part, c, k, 1] = wa * after + za * u1[it, part, k, 1]

    for load in loads:
        load.wait()
    pack(0)
    edge_sums(0)
    stencil(0, 0, False)
    pl.semaphore_wait(barrier, 2 * nz + 1 + has_left.astype(jnp.int32) + has_right.astype(jnp.int32))
    send_halo(0, 0)
    send_halo(0, 1)
    for it in range(ITERS):
        up_core(it, 0)
        stencil(it, 1, False)
        up_owner(it, 0)
        wait_halo(it, 0)
        mend_outer_sums(it)
        up_core(it, 1)
        if it > 0:
            mend_inner(it)
        up_owner(it, 1)
        wait_halo(it, 1)
        mend_outer(it)
        down_owner(it, 0)
        down_owner(it, 1)
        down_core(it, 0)
        arrive(yv.at[it, 0, 1 - c], it, 0, back)
        solve(it, 0, (0, 1))
        if it + 1 < ITERS:
            stencil(it + 1, 0, True)
        down_core(it, 1)
        for own in (True, False):
            if not own:
                arrive(yv.at[it, 1, 1 - c], it, 1, back)
            pl.when(first == own)(lambda: solve(it, 1, (0,)))
            pl.when(first != own)(lambda: solve(it, 1, (1,)))
        if it + 1 < ITERS:
            send_halo(it + 1, 0)
            send_halo(it + 1, 1)
    for one_copy in pending:
        one_copy.wait_send()
    for it in range(ITERS):
        for kind in range(2):
            pl.when(has_right)(lambda: halo(it, 0, kind).wait_send())
            pl.when(has_left)(lambda: halo(it, 1, kind).wait_send())


def solution(mesh):
    nz = mesh.shape["tm"] // 4
    ny = mesh.shape["space"] // 2

    def on_device(field, step, mass):
        slices, planes, width = field.shape
        tiles = width // LANES
        tile = (ROWS, LANES)
        vmem = lambda *shape: pltpu.VMEM(shape, jnp.float32)
        level = (ITERS, 2)
        sems = 2 + 4 * nz
        return pl.pallas_call(
            functools.partial(kernel, nz, ny, slices),
            out_shape=jax.ShapeDtypeStruct(field.shape, field.dtype),
            in_specs=[
                pl.BlockSpec(memory_space=pltpu.SMEM),
                pl.BlockSpec(memory_space=pltpu.SMEM),
                pl.BlockSpec(memory_space=pltpu.HBM),
            ],
            out_specs=pl.BlockSpec(memory_space=pltpu.VMEM),
            scratch_shapes=[
                vmem(slices, tiles + 2, planes + 2 * ROWS, LANES),
                vmem(slices, tiles, planes, LANES),
                vmem(ITERS, 2, slices, tiles, LANES),
                vmem(ITERS, 2, slices, tiles, LANES),
                vmem(ITERS, 2, 2, tiles, LANES),
                vmem(ITERS, 2, 2, tiles, LANES),
                vmem(*level, 2, tiles, 2, *tile),
                vmem(*level, tiles, 2, *tile),
                vmem(*level, tiles, 2, *tile),
                vmem(*level, tiles, 2, *tile),
                vmem(*level, tiles, 2, *tile),
                vmem(*level, tiles, 2, *tile),
                vmem(*level, tiles, 2, *tile),
                vmem(*level, 2, tiles, 2, *tile),
                pltpu.SemaphoreType.DMA((tiles,)),
                pltpu.SemaphoreType.DMA((*level, sems)),
                pltpu.SemaphoreType.DMA((*level, sems)),
                pltpu.SemaphoreType.DMA((ITERS, 2, 2)),
                pltpu.SemaphoreType.DMA((ITERS, 2, 2)),
            ],
            compiler_params=pltpu.CompilerParams(
                collective_id=0, has_side_effects=True, vmem_limit_bytes=VMEM_MIB * 1024 * 1024
            ),
        )(step, mass, pltpu.with_memory_space_constraint(field, pltpu.HBM))

    return jax.shard_map(
        on_device,
        mesh=mesh,
        in_specs=(P("tm", "space", None), P(), P()),
        out_specs=P("tm", "space", None),
        check_vma=False,
    )
```

```python
import functools

import jax
import jax.numpy as jnp
from jax import lax
from jax.experimental import pallas as pl
from jax.experimental.pallas import tpu as pltpu
from jax.sharding import PartitionSpec as P

NZ = 32
ITERS = 2
VMEM_MIB = 40
LANES = 128
ROWS = 8
MESH = pl.DeviceIdType.MESH


def kernel(nz, ny, slices, step_ref, mass_ref, field, out, fb, gb, hs, hb, hq, hm, mom, u1, xs, zr, ws, wr, cs, yv,
           load_sem, send, recv, hsend, hrecv, qsend, qrecv):
    tiles = fb.shape[1] - 2
    groups = fb.shape[2] // ROWS - 2
    tm, sp = lax.axis_index("tm"), lax.axis_index("space")
    z, h, c = tm // 4, (tm // 2) % 2, tm % 2
    lo, y = sp // ny, sp % ny
    last = 2 * ny - 1
    other = (tm + 1 - 2 * c, sp)
    owner = lambda d, hd: (((z + d) % nz) * 4 + hd * 2 + c, (1 - lo) * ny + y)
    has_left, has_right = sp > 0, sp < last

    barrier = pltpu.get_barrier_semaphore()

    def greet(device):
        pl.semaphore_signal(barrier, inc=1, device_id=device, device_id_type=MESH)

    far_first = sorted(range(nz), key=lambda d: (-min(d, nz - d), d))
    for d in far_first:
        for hd in range(2):
            greet(owner(d, hd))
    greet(other)
    has_mine = jnp.where(c == 0, has_left, has_right)
    pl.when(has_mine)(lambda: greet((tm + 1 - 2 * c, sp - 1 + 2 * c)))

    @pl.when(has_left)
    def _():
        greet((tm, sp - 1))

    @pl.when(has_right)
    def _():
        greet((tm, sp + 1))

    loads = [
        pltpu.make_async_copy(
            field.at[:, :, pl.ds(k * LANES, LANES)],
            fb.at[:, k + 1, pl.ds(ROWS, groups * ROWS), :],
            load_sem.at[k],
        )
        for k in range(tiles)
    ]
    for load in loads:
        load.start()

    full = lambda value: jnp.full((ROWS, LANES), value, jnp.float32)
    blank = full(0.0)

    @pl.loop(0, slices)
    def _(t):
        for k in (0, tiles + 1):
            for i in range(groups):
                fb[t, k, pl.ds((i + 1) * ROWS, ROWS), :] = blank
        for k in range(tiles):
            fb[t, k + 1, pl.ds(0, ROWS), :] = blank
            fb[t, k + 1, pl.ds((groups + 1) * ROWS, ROWS), :] = blank

    def clear(which):
        for it in range(ITERS):
            hb[it, which] = jnp.zeros(hb.shape[2:], jnp.float32)

    @pl.when(jnp.logical_not(has_mine))
    def _():
        hm[...] = jnp.zeros(hm.shape, jnp.float32)

    pl.when(jnp.logical_not(has_left))(lambda: clear(0))
    pl.when(jnp.logical_not(has_right))(lambda: clear(1))

    m = full(mass_ref[0])
    s = full(step_ref[0])
    m2 = m * m
    q = m * jnp.sqrt(1.0 + 0.25 * m2) - 0.5 * m2
    double = lambda p: p * (2.0 - p)
    r = 1.0 - q
    q8 = double(double(double(q)))
    q16 = double(q8)
    r8, r16 = 1.0 - q8, 1.0 - q16
    whole = q16
    for _ in range((2 * nz - 1).bit_length()):
        whole = double(whole)
    inv = 1.0 / whole
    linear = 7.0 - m2
    keep = 1.0 - s
    gain = s * r / (q * (1.0 + r))
    first = c == 0
    one = full(1.0)
    wa, wb = jnp.where(first, r8, one), jnp.where(first, one, r8)
    za, zb = jnp.where(first, one, blank), jnp.where(first, blank, one)

    lane = lax.broadcasted_iota(jnp.int32, (ROWS, LANES), 1)
    row = lax.broadcasted_iota(jnp.int32, (ROWS, LANES), 0)
    zplace = lane % NZ
    at_first, at_last = zplace == 0, zplace == NZ - 1
    low, high = lane < NZ, lane >= LANES - NZ
    top, bottom = row == 0, row == ROWS - 1

    parts = (tuple(range(1, groups - 1)), (0, groups - 1))

    def stencil(it, part, lacks):
        @pl.loop(0, tiles // 4)
        def _(quad):
            for k in (quad * 4 + j for j in range(4)):
                for half, i in enumerate(parts[part]):
                    rows = pl.ds((i + 1) * ROWS, ROWS)
                    gs = []
                    for t in range(slices):
                        f = fb[t, k + 1, rows, :]
                        xm = fb[t, k + 1, pl.ds((i + 1) * ROWS - 1, ROWS), :]
                        xp = fb[t, k + 1, pl.ds((i + 1) * ROWS + 1, ROWS), :]
                        if lacks and half == 0:
                            xm = jnp.where(top, 0.0, xm)
                        if lacks and half == 1:
                            xp = jnp.where(bottom, 0.0, xp)
                        yp = pltpu.roll(jnp.where(low, fb[t, k + 2, rows, :], f), LANES - NZ, 1)
                        ym = pltpu.roll(jnp.where(high, fb[t, k, rows, :], f), NZ, 1)
                        zp = pltpu.roll(jnp.where(at_first, 0.0, f), LANES - 1, 1)
                        zm = pltpu.roll(jnp.where(at_last, 0.0, f), 1, 1)
                        near = (xm + xp) + (yp + ym) + (zp + zm)
                        g = f * (linear + f * (0.25 * f - 0.9)) - near
                        gb[t, k, pl.ds(i * ROWS, ROWS), :] = g
                        gs.append(g)
                    before, after = gs[0], gs[-1]
                    for t in range(1, slices):
                        before = r * before + gs[t]
                        after = r * after + gs[slices - 1 - t]
                    mom[it, part, half, k, 0] = before
                    mom[it, part, half, k, 1] = after

    edges = (top, bottom)
    edge = row == c * (ROWS - 1)

    def edge_sums(it):
        for side in range(2):
            for lo_k in range(0, tiles, ROWS):
                band = pl.ds(lo_k, ROWS)
                planes = [hs[it, side, t, band, :] for t in range(slices)]
                before, after = planes[0], planes[-1]
                for t in range(1, slices):
                    before = r * before + planes[t]
                    after = r * after + planes[slices - 1 - t]
                hq[it, side, 0, band, :] = before
                hq[it, side, 1, band, :] = after

    def mend_outer_sums(it):
        for k in range(tiles):
            line = pl.ds(k, 1)
            for which in range(2):
                own = jnp.where(edge, hm[it, c, which, line, :], 0.0)
                theirs = jnp.where(edge, hm[it, 1 - c, which, line, :], 0.0)
                mom[it, 1, c, k, which] = mom[it, 1, c, k, which] - own
                u1[it, 1, k, which] = u1[it, 1, k, which] - theirs

    def mend_outer(it):
        @pl.loop(0, slices)
        def _(t):
            for half, i in enumerate(parts[1]):
                rows = pl.ds(i * ROWS, ROWS)
                for k in range(tiles):
                    add = jnp.where(edges[half], hb[it, half, t, pl.ds(k, 1), :], 0.0)
                    gb[t, k, rows, :] = gb[t, k, rows, :] - add

    def mend_inner(it):
        @pl.loop(0, slices)
        def _(t):
            for half, i in enumerate(parts[0]):
                rows = pl.ds(i * ROWS, ROWS)
                for k in range(tiles):
                    shifted = fb[t, k + 1, pl.ds((i + 1) * ROWS + 2 * half - 1, ROWS), :]
                    gb[t, k, rows, :] = gb[t, k, rows, :] - jnp.where(edges[half], shifted, 0.0)

    def solve(it, part, halves):
        @pl.loop(0, tiles // 4)
        def _(quad):
            for j in range(4):
                k = quad * 4 + j
                for half in halves:
                    i = parts[part][half]
                    rows = pl.ds((i + 1) * ROWS, ROWS)
                    gs = [gb[t, k, pl.ds(i * ROWS, ROWS), :] for t in range(slices)]
                    state = yv[it, part, half, k, 0]
                    states = []
                    for t in range(slices):
                        state = r * state + gs[t]
                        states.append(state)
                    ahead = r * yv[it, part, half, k, 1]
                    news = [None] * slices
                    for t in reversed(range(slices)):
                        new = keep * fb[t, k + 1, rows, :] - gain * (states[t] + ahead)
                        ahead = r * (gs[t] + ahead)
                        news[t] = new
                        if it + 1 < ITERS:
                            fb[t, k + 1, rows, :] = new
                        else:
                            out[t, pl.ds(i * ROWS, ROWS), pl.ds(pl.multiple_of(k * LANES, LANES), LANES)] = new
                        if it + 1 < ITERS and part == 1:
                            edge = half * (ROWS - 1)
                            hs[it + 1, 1 - half, t, pl.ds(k, 1), :] = new[edge : edge + 1]
                    if it + 1 < ITERS and part == 1:
                        before, after = news[0], news[-1]
                        for t in range(1, slices):
                            before = r * before + news[t]
                            after = r * after + news[slices - 1 - t]
                        turn, at = (1, ROWS - 1)[half], half * (ROWS - 1)
                        for which, add in enumerate((before, after)):
                            hq[it + 1, 1 - half, which, pl.ds(k, 1), :] = add[at : at + 1]
                            add = jnp.where(edges[half], pltpu.roll(add, turn, 0), 0.0)
                            mom[it + 1, 0, half, k, which] = mom[it + 1, 0, half, k, which] - add

    pending = []

    def copy(src, dst, send_sem, recv_sem, device):
        return pltpu.make_async_remote_copy(
            src_ref=src, dst_ref=dst, send_sem=send_sem, recv_sem=recv_sem, device_id=device, device_id_type=MESH
        )

    def start(src, dst, it, part, a, b, device):
        one_copy = copy(src, dst, send.at[it, part, a], recv.at[it, part, b], device)
        one_copy.start()
        pending.append(one_copy)

    def arrive(dst, it, part, b):
        copy(dst, dst, send.at[it, part, b], recv.at[it, part, b], other).wait_recv()

    def pack(it):
        @pl.loop(0, slices)
        def _(t):
            for which, edge in enumerate((groups * ROWS - 1, 0)):
                for k in range(tiles):
                    hs[it, which, t, pl.ds(k, 1), :] = fb[t, k + 1, pl.ds(ROWS + edge, 1), :]

    def halo(it, which):
        return copy(
            hs.at[it, which],
            hb.at[it, which],
            hsend.at[it, which],
            hrecv.at[it, which],
            (tm, sp + 1) if which == 0 else (tm, sp - 1),
        )

    def halo_sums(it, which, source):
        return copy(
            hq.at[it, which],
            hm.at[it, source],
            qsend.at[it, which],
            qrecv.at[it, source],
            (tm - c + which, sp + 1 - 2 * which),
        )

    def send_halo(it):
        pl.when(has_right)(lambda: halo_sums(it, 0, c).start())
        pl.when(has_left)(lambda: halo_sums(it, 1, c).start())
        pl.when(has_right)(lambda: halo(it, 0).start())
        pl.when(has_left)(lambda: halo(it, 1).start())

    def wait_sums(it):
        for source in range(2):
            pl.when(has_mine)(lambda: halo_sums(it, 0, source).wait_recv())

    def wait_halo(it):
        pl.when(has_left)(lambda: halo(it, 0).wait_recv())
        pl.when(has_right)(lambda: halo(it, 1).wait_recv())

    up = lambda d, hd: 1 + 2 * d + hd
    down = lambda d, hd: 1 + 2 * nz + 2 * d + hd
    back = 1 + 4 * nz

    def up_core(it, part):
        start(mom.at[it, part, 1 - c], u1.at[it, part], it, part, 0, 0, other)

    def up_owner(it, part):
        arrive(u1.at[it, part], it, part, 0)
        if part == 1:
            wait_sums(it)
            mend_outer_sums(it)
        for k in range(tiles):
            xs[it, part, k, 0] = wa * mom[it, part, c, k, 0] + wb * u1[it, part, k, 0]
            xs[it, part, k, 1] = wb * mom[it, part, c, k, 1] + wa * u1[it, part, k, 1]
        for d in far_first:
            for hd in range(2):
                src = xs.at[it, part, hd * nz + (z + d) % nz]
                start(src, zr.at[it, part, z * 2 + h], it, part, up(d, hd), up(d, h), owner(d, hd))

    def down_owner(it, part):
        for d in reversed(far_first):
            for hd in range(2):
                arrive(zr.at[it, part, ((z + nz - d) % nz) * 2 + hd], it, part, up(d, hd))
        ms = [zr[it, part, j, 0] for j in range(2 * nz)]
        ns = [zr[it, part, j, 1] for j in range(2 * nz)]
        left, right, ratio = ms, ns, r16
        while len(left) > 1:
            pairs = range(0, len(left), 2)
            left = [ratio * left[j] + left[j + 1] for j in pairs]
            right = [right[j] + ratio * right[j + 1] for j in pairs]
            ratio = ratio * ratio
        before, after = inv * left[0], inv * right[0]
        for j in range(2 * nz):
            ws[it, part, j, 0] = before
            ws[it, part, 2 * nz - 1 - j, 1] = after
            before = r16 * before + ms[j]
            after = r16 * after + ns[2 * nz - 1 - j]
        for d in far_first:
            for hd in range(2):
                src = ws.at[it, part, ((z + d) % nz) * 2 + hd]
                start(src, wr.at[it, part, h * nz + z], it, part, down(d, hd), down(d, h), owner(d, hd))

    def down_core(it, part):
        for d in reversed(far_first):
            for hd in range(2):
                arrive(wr.at[it, part, hd * nz + (z + nz - d) % nz], it, part, down(d, hd))
        for k in range(tiles):
            before, after = wr[it, part, k, 0], wr[it, part, k, 1]
            cs[it, part, k, 0] = wa * before + za * mom[it, part, c, k, 0]
            cs[it, part, k, 1] = wb * after + zb * mom[it, part, c, k, 1]
        start(cs.at[it, part], yv.at[it, part, c], it, part, back, back, other)
        for k in range(tiles):
            before, after = wr[it, part, k, 0], wr[it, part, k, 1]
            yv[it, part, c, k, 0] = wb * before + zb * u1[it, part, k, 0]
            yv[it, part, c, k, 1] = wa * after + za * u1[it, part, k, 1]

    for load in loads:
        load.wait()
    pack(0)
    edge_sums(0)
    stencil(0, 0, False)
    pl.semaphore_wait(barrier, 2 * nz + 1 + has_left.astype(jnp.int32) + has_right.astype(jnp.int32) + has_mine.astype(jnp.int32))
    send_halo(0)
    for it in range(ITERS):
        up_core(it, 0)
        stencil(it, 1, False)
        up_core(it, 1)
        up_owner(it, 0)
        if it > 0:
            mend_inner(it)
        up_owner(it, 1)
        wait_halo(it)
        mend_outer(it)
        down_owner(it, 0)
        down_owner(it, 1)
        down_core(it, 0)
        arrive(yv.at[it, 0, 1 - c], it, 0, back)
        solve(it, 0, (0, 1))
        if it + 1 < ITERS:
            stencil(it + 1, 0, True)
        down_core(it, 1)
        for own in (True, False):
            if not own:
                arrive(yv.at[it, 1, 1 - c], it, 1, back)
            pl.when(first == own)(lambda: solve(it, 1, (0,)))
            pl.when(first != own)(lambda: solve(it, 1, (1,)))
        if it + 1 < ITERS:
            send_halo(it + 1)
    for one_copy in pending:
        one_copy.wait_send()
    for it in range(ITERS):
        for kind in (halo, lambda it, which: halo_sums(it, which, c)):
            pl.when(has_right)(lambda: kind(it, 0).wait_send())
            pl.when(has_left)(lambda: kind(it, 1).wait_send())


def solution(mesh):
    nz = mesh.shape["tm"] // 4
    ny = mesh.shape["space"] // 2

    def on_device(field, step, mass):
        slices, planes, width = field.shape
        tiles = width // LANES
        tile = (ROWS, LANES)
        vmem = lambda *shape: pltpu.VMEM(shape, jnp.float32)
        level = (ITERS, 2)
        sems = 2 + 4 * nz
        return pl.pallas_call(
            functools.partial(kernel, nz, ny, slices),
            out_shape=jax.ShapeDtypeStruct(field.shape, field.dtype),
            in_specs=[
                pl.BlockSpec(memory_space=pltpu.SMEM),
                pl.BlockSpec(memory_space=pltpu.SMEM),
                pl.BlockSpec(memory_space=pltpu.HBM),
            ],
            out_specs=pl.BlockSpec(memory_space=pltpu.VMEM),
            scratch_shapes=[
                vmem(slices, tiles + 2, planes + 2 * ROWS, LANES),
                vmem(slices, tiles, planes, LANES),
                vmem(ITERS, 2, slices, tiles, LANES),
                vmem(ITERS, 2, slices, tiles, LANES),
                vmem(ITERS, 2, 2, tiles, LANES),
                vmem(ITERS, 2, 2, tiles, LANES),
                vmem(*level, 2, tiles, 2, *tile),
                vmem(*level, tiles, 2, *tile),
                vmem(*level, tiles, 2, *tile),
                vmem(*level, tiles, 2, *tile),
                vmem(*level, tiles, 2, *tile),
                vmem(*level, tiles, 2, *tile),
                vmem(*level, tiles, 2, *tile),
                vmem(*level, 2, tiles, 2, *tile),
                pltpu.SemaphoreType.DMA((tiles,)),
                pltpu.SemaphoreType.DMA((*level, sems)),
                pltpu.SemaphoreType.DMA((*level, sems)),
                pltpu.SemaphoreType.DMA((ITERS, 2)),
                pltpu.SemaphoreType.DMA((ITERS, 2)),
                pltpu.SemaphoreType.DMA((ITERS, 2)),
                pltpu.SemaphoreType.DMA((ITERS, 2)),
            ],
            compiler_params=pltpu.CompilerParams(
                collective_id=0, has_side_effects=True, vmem_limit_bytes=VMEM_MIB * 1024 * 1024
            ),
        )(step, mass, pltpu.with_memory_space_constraint(field, pltpu.HBM))

    return jax.shard_map(
        on_device,
        mesh=mesh,
        in_specs=(P("tm", "space", None), P(), P()),
        out_specs=P("tm", "space", None),
        check_vma=False,
    )
```
